256 devices in a mesh: grp: 32 (over x, y, core), tp: 8 (over z).
Axes of the slice: x: 4, y: 4, z: 8, core: 2. Of those that a mesh axis runs over, the one named last changes fastest.
Arguments:
- hidden_in: bfloat16 [512, 2048], P('grp'), may hold values from -6 to 6
- norm_gain: bfloat16 [2048], replicated, may hold values from 0.099609375 to 1.8984375
- w_query: bfloat16 [2048, 2048], P(None, 'tp'), may hold values from -0.125 to 0.125
- w_keyval: bfloat16 [2048, 512], P(None, 'tp'), may hold values from -0.125 to 0.125
- w_output: bfloat16 [2048, 2048], P('tp'), may hold values from -0.125 to 0.125
- prefix_cache: bfloat16 [64, 512, 512], P('grp', 'tp'), may hold values from -130 to 130
- private_cache: bfloat16 [512, 512, 512], P('grp', 'tp'), may hold values from -130 to 130
- node_parent: int32 [64], replicated, may hold values from 0 to 3, as said below
- node_length: int32 [64], replicated, may hold values from 1 to 512, as said below
- request_node: int32 [512], replicated, may hold values from 4 to 63, as said below
- private_length: int32 [512], P('grp'), may hold values from 0 to 512, as said below
Outputs:
- hidden_out: bfloat16 [512, 2048], P('grp', 'tp')
- new_keyval: bfloat16 [512, 512], P('grp', 'tp')
The draws below stay inside these ranges and needn't reach their ends.
Inputs may be any that keep to these rules, and one draw needn't show every extreme that they name: `node_parent`: nodes 0 to 3 are the tenants' roots and are their own parents; every other node's parent is a root, and every root has a child. `request_node`: request r belongs to tenant r // 128; its node is a non-root node whose parent is that tenant's root. `node_length`: the longest node has exactly 512 used slots. `private_length`: some request has exactly 512 used slots.
All inputs are finite; a program needn't handle non-finite values.
Results may differ from the reference program's by a relative error of at most 0.023.
Values may be sent and summed in bfloat16 or wider, within the bound.
A program may use at most 128 MiB of HBM per device.

```python
import math
import jax
import jax.numpy as jnp
from jax import lax

D = 2048
HEADS = 32
KV_HEADS = 4
HEAD_DIM = 64
TENANTS = 4
PLEN = 512
CLEN = 512
REQS = 512
NODES = 64
PER_TENANT = 128


def cache_draw(seed_key, row_total, length):
    width = 2 * KV_HEADS * HEAD_DIM
    key_width = KV_HEADS * HEAD_DIM
    column = jnp.arange(width)[None, None, :]
    normal_rows = jax.random.truncated_normal(jax.random.fold_in(seed_key, 1), -4.0, 4.0, (row_total, length, width))
    result = normal_rows * jnp.where(column < key_width, 2.5, 1.0)
    return result.astype(jnp.bfloat16)


def tree_draw(seed_key):
    node_ids = jnp.arange(NODES)
    random_parent = jax.random.randint(jax.random.fold_in(seed_key, 11), (NODES,), 0, TENANTS)
    parents = jnp.where(node_ids < TENANTS, node_ids, jnp.where(node_ids < 2 * TENANTS, node_ids - TENANTS, random_parent)).astype(jnp.int32)
    scores = jax.random.randint(jax.random.fold_in(seed_key, 12), (REQS, NODES), 0, 1 << 20) * NODES + node_ids[None, :]
    tenant = jnp.arange(REQS) // PER_TENANT
    allowed = (parents[None, :] == tenant[:, None]) & (node_ids[None, :] >= TENANTS)
    scores = jnp.where(allowed, scores, -1).astype(jnp.int32)
    chosen = lax.top_k(scores, 1)[1][:, 0].astype(jnp.int32)
    return (parents, chosen)


def draw_prefix_cache(key, part):
    return cache_draw(key, NODES, PLEN)


def draw_private_cache(key, part):
    return cache_draw(jax.random.fold_in(key, 5), REQS, CLEN)


def draw_node_parent(key, part):
    return tree_draw(key)[0]


def draw_request_node(key, part):
    return tree_draw(key)[1]


def draw_node_length(key, part):
    lengths = jax.random.randint(jax.random.fold_in(key, 21), (NODES,), 1, PLEN + 1)
    longest = jax.random.randint(jax.random.fold_in(key, 22), (), 0, NODES)
    return jnp.where(jnp.arange(NODES) == longest, PLEN, lengths).astype(jnp.int32)


def draw_private_length(key, part):
    lengths = jax.random.randint(jax.random.fold_in(key, 31), (REQS,), 0, CLEN + 1)
    longest = jax.random.randint(jax.random.fold_in(key, 32), (), 0, REQS)
    return jnp.where(jnp.arange(REQS) == longest, CLEN, lengths).astype(jnp.int32)


def levels(key, dims, pieces, smallest, largest):
    factor_of, own = 1.0, jax.random.fold_in(key, 6)
    for axis_at, shards_of in pieces:
        draws = jnp.exp(jax.random.uniform(jax.random.fold_in(own, axis_at), (shards_of,), jnp.float32, smallest / len(pieces), largest / len(pieces)))
        factor_of = factor_of * jnp.repeat(draws, dims[axis_at] // shards_of).reshape([-1 if axis == axis_at else 1 for axis in range(len(dims))])
    return factor_of


def bell_draw(key, dims, scale, limit, pieces=(), kind=jnp.bfloat16):
    entries = scale * jax.random.normal(key, dims, jnp.float32)
    if pieces:
        entries = entries * levels(key, dims, pieces, -0.22, 0.18)
    return jnp.clip(entries, -limit, limit).astype(kind)


def setup_inputs(seed: int = 0) -> dict:
    arg_keys = jax.random.split(jax.random.key(seed), 12)
    hidden_in = bell_draw(arg_keys[0], (REQS, D), 1.0, 6.0, ((0, 32),))
    norm_gain = jnp.clip(1.0 + 0.18 * jax.random.normal(arg_keys[1], (D,), jnp.float32), 0.099609375, 1.8984375).astype(jnp.bfloat16)
    w_query = bell_draw(arg_keys[2], (D, HEADS * HEAD_DIM), D ** -0.5, 0.125, ((1, 8),))
    w_keyval = bell_draw(arg_keys[3], (D, 2 * KV_HEADS * HEAD_DIM), D ** -0.5, 0.125, ((1, 8),))
    w_output = bell_draw(arg_keys[4], (HEADS * HEAD_DIM, D), (HEADS * HEAD_DIM) ** -0.5, 0.125, ((0, 8),))
    prefix_cache = draw_prefix_cache(jax.random.fold_in(arg_keys[11], 71), 0)
    private_cache = draw_private_cache(jax.random.fold_in(arg_keys[11], 71), 0)
    node_parent = draw_node_parent(jax.random.fold_in(arg_keys[11], 71), 0)
    node_length = draw_node_length(jax.random.fold_in(arg_keys[11], 71), 0)
    request_node = draw_request_node(jax.random.fold_in(arg_keys[11], 71), 0)
    private_length = draw_private_length(jax.random.fold_in(arg_keys[11], 71), 0)
    return dict(hidden_in=hidden_in, norm_gain=norm_gain, w_query=w_query, w_keyval=w_keyval, w_output=w_output, prefix_cache=prefix_cache, private_cache=private_cache, node_parent=node_parent, node_length=node_length, request_node=request_node, private_length=private_length)


def rms_norm(values, scale_gain):
    floats = values.astype(jnp.float32)
    spread = lax.optimization_barrier(jnp.mean(floats * floats, axis=-1, keepdims=True))
    return (floats * lax.rsqrt(spread + 1e-05) * scale_gain.astype(jnp.float32)).astype(jnp.bfloat16)

def rotate(head_rows, position):
    half_dim = head_rows.shape[-1] // 2
    freq_index = jnp.arange(half_dim, dtype=jnp.float32)
    frequency = jnp.exp(freq_index * (-2.0 * math.log(10000.0) / head_rows.shape[-1]))
    angles = position[:, None, None] * frequency[None, None, :]
    cosine = jnp.cos(angles)
    sine_part = jnp.sin(angles)
    front_half = head_rows[..., :half_dim]
    back_half = head_rows[..., half_dim:]
    return jnp.concatenate([front_half * cosine - back_half * sine_part, back_half * cosine + front_half * sine_part], axis=-1)

def reference(hidden_in, norm_gain, w_query, w_keyval, w_output, prefix_cache, private_cache, node_parent, node_length, request_node, private_length):
    share_count = HEADS // KV_HEADS
    key_width = KV_HEADS * HEAD_DIM
    normed = rms_norm(hidden_in, norm_gain)
    query = jnp.dot(normed, w_query, preferred_element_type=jnp.float32)
    keyval = jnp.dot(normed, w_keyval, preferred_element_type=jnp.float32)
    root_node = node_parent[request_node]
    position = (node_length[root_node] + node_length[request_node] + private_length).astype(jnp.float32)
    query_rot = rotate(query.reshape(REQS, HEADS, HEAD_DIM), position).reshape(REQS, HEADS * HEAD_DIM).astype(jnp.bfloat16)
    kv_rows = keyval.reshape(REQS, 2 * KV_HEADS, HEAD_DIM)
    key_rot = rotate(kv_rows[:, :KV_HEADS], position)
    new_keyval = jnp.concatenate([key_rot, kv_rows[:, KV_HEADS:]], axis=1).reshape(REQS, 2 * key_width).astype(jnp.bfloat16)

    def one_request(request):
        root_id = root_node[request]
        mid_id = request_node[request]
        rows_all = jnp.concatenate([prefix_cache[root_id], prefix_cache[mid_id], private_cache[request], new_keyval[request][None, :]], axis=0)
        valid = jnp.concatenate([jnp.arange(PLEN) < node_length[root_id], jnp.arange(PLEN) < node_length[mid_id], jnp.arange(CLEN) < private_length[request], jnp.ones((1,), dtype=bool)])
        total_len = rows_all.shape[0]
        key_rows = rows_all[:, :key_width].reshape(total_len, KV_HEADS, HEAD_DIM).astype(jnp.float32)
        value_rows = rows_all[:, key_width:].reshape(total_len, KV_HEADS, HEAD_DIM).astype(jnp.float32)
        grouped = query_rot[request].reshape(KV_HEADS, share_count, HEAD_DIM).astype(jnp.float32)
        scores = jnp.einsum('kgd,lkd->kgl', grouped, key_rows) * HEAD_DIM ** (-0.5)
        scores = jnp.where(valid[None, None, :], scores, -jnp.inf)
        maxima = lax.optimization_barrier(jnp.max(scores, axis=-1, keepdims=True))
        weights = jnp.exp(scores - maxima)
        totals = lax.optimization_barrier(jnp.sum(weights, axis=-1))
        rounded = lax.optimization_barrier(weights.astype(jnp.bfloat16))
        weighted = jnp.einsum('kgl,lkd->kgd', rounded.astype(jnp.float32), value_rows)
        return (weighted / totals[..., None]).reshape(HEADS * HEAD_DIM)
    attention = lax.map(one_request, jnp.arange(REQS)).astype(jnp.bfloat16)
    projected = jnp.dot(attention, w_output, preferred_element_type=jnp.float32)
    hidden_out = (projected + hidden_in.astype(jnp.float32)).astype(jnp.bfloat16)
    return (hidden_out, new_keyval)
```

```python
import math

import jax
import jax.numpy as jnp
from jax import lax
from jax.experimental import pallas as pl
from jax.experimental.pallas import tpu as pltpu
from jax.sharding import PartitionSpec as P

MESH = pl.DeviceIdType.MESH
F32 = jnp.float32
BF16 = jnp.bfloat16
HEADS = 32
KV_HEADS = 4
HEAD_DIM = 64
REQ = 16
SLOTS = 64
ROWS = HEADS * REQ
KW = KV_HEADS * HEAD_DIM
LOW = -1e30


def dot(a, b):
    return jnp.dot(a, b, preferred_element_type=F32)


def dot_t(a, b):
    return lax.dot_general(a, b, (((1,), (1,)), ((), ())), preferred_element_type=F32)


def three_parts(value):
    first = value.astype(BF16).astype(F32)
    rest = value - first
    second = rest.astype(BF16).astype(F32)
    third = (rest - second).astype(BF16).astype(F32)
    return first, second, third


def rope_tables(position):
    lane = lax.broadcasted_iota(jnp.int32, (REQ, 128), 1)
    index = (lane % (HEAD_DIM // 2)).astype(F32)
    frequency = jnp.exp(index * (-2.0 * math.log(10000.0) / HEAD_DIM))
    angle = position * frequency
    front = lane % HEAD_DIM < HEAD_DIM // 2
    sine = jnp.sin(angle)
    return jnp.cos(angle), jnp.where(front, -sine, sine), front


def rope(block, tables):
    cosine, sine, front = tables
    half = HEAD_DIM // 2
    swapped = jnp.where(front, pltpu.roll(block, 128 - half, 1), pltpu.roll(block, half, 1))
    return block * cosine + swapped * sine


def kernel(
    hid, gain, wq, wkv, wo, prefix, private, parent, nlen, reqnode, plen,
    out_h, out_kv,
    v_hid, v_gain, v_wq, v_wkv, v_wo, v_priv, nodes,
    q_all, kv_send, kv_recv, part_send, part_recv, rs_send, rs_recv,
    l_sem, a_send, a_recv, d_send, d_recv, s_send, s_recv, z_send, z_recv, kv_ss, kv_rs,
):
    g = lax.axis_index("grp")
    t = lax.axis_index("tp")
    x, y, c = g // 8, (g // 2) % 4, g % 2

    def group(xx, yy, cc):
        return (xx * 4 + yy) * 2 + cc

    def chunk(xx, yy, cc):
        return nodes.at[pl.ds(group(xx, yy, cc) * 2, 2)]

    def half_chunk(xx, yy, cc, i):
        return nodes.at[pl.ds(group(xx, yy, cc) * 2 + i, 1)]

    x_peer = [(group((x + d) % 4, y, c), t) for d in range(4)]
    y_peer = [(group(x, (y + d) % 4, c), t) for d in range(4)]
    sibling = (group(x, y, 1 - c), t)
    z_peer = [(g, (t + d) % 8) for d in range(8)]
    everyone = x_peer[1:] + y_peer[1:] + [sibling] + z_peer[1:]

    barrier = pltpu.get_barrier_semaphore()
    for peer in everyone:
        pl.semaphore_signal(barrier, inc=1, device_id=peer, device_id_type=MESH)

    locals_ = []
    for k, (src, dst) in enumerate(
        ((hid, v_hid), (gain, v_gain), (wq, v_wq), (wkv, v_wkv), (private, v_priv), (wo, v_wo),
         (prefix, chunk(x, y, c)))
    ):
        copy = pltpu.make_async_copy(src, dst, l_sem.at[k])
        copy.start()
        locals_.append(copy)

    pl.semaphore_wait(barrier, len(everyone))

    sends = []

    def send(src, dst, ssem, rsem, peer):
        copy = pltpu.make_async_remote_copy(
            src_ref=src, dst_ref=dst, send_sem=ssem, recv_sem=rsem, device_id=peer, device_id_type=MESH
        )
        copy.start()
        sends.append(copy)

    def arrived(ref, sem):
        pltpu.make_async_copy(ref, ref, sem).wait()

    own = chunk(x, y, c)
    for d in (1, 3, 2):
        send(prefix, own, a_send.at[0, d], a_recv.at[0, d], x_peer[d])
        send(prefix, own, a_send.at[1, d], a_recv.at[1, d], y_peer[d])
    send(prefix, own, s_send.at[0, 0], s_recv.at[0, 0], sibling)

    mids = [reqnode[g * REQ + r] for r in range(REQ)]
    root = parent[mids[0]]
    root_length = nlen[root]
    row16 = lax.broadcasted_iota(jnp.int32, (REQ, 128), 0)
    lane16 = lax.broadcasted_iota(jnp.int32, (REQ, 128), 1)
    private_length = jnp.zeros((REQ, 128), jnp.int32)
    mid_length = jnp.zeros((REQ, 128), jnp.int32)
    for r in range(REQ):
        private_length = jnp.where(row16 == r, plen[r], private_length)
        mid_length = jnp.where(row16 == r, nlen[mids[r]], mid_length)
    tables = rope_tables((private_length + mid_length + root_length).astype(F32))

    locals_[0].wait()
    locals_[1].wait()
    floats = v_hid[...].astype(F32)
    spread = jnp.mean(floats * floats, axis=-1, keepdims=True)
    normed = (floats * lax.rsqrt(spread + 1e-05) * v_gain[...].astype(F32)).astype(BF16)
    locals_[2].wait()
    query = dot(normed, v_wq[...])
    for half in range(2):
        piece = rope(query[:, half * 128 : half * 128 + 128], tables).astype(BF16)
        q_all[t, :, half * 128 : half * 128 + 128] = piece * jnp.asarray(HEAD_DIM**-0.5, BF16)
    for d in (4, 3, 5, 2, 6, 1, 7):
        send(q_all.at[t], q_all.at[t], z_send.at[0, d], z_recv.at[0, d], z_peer[d])

    locals_[3].wait()
    keyval = dot(normed, v_wkv[...])
    doubled = jnp.concatenate([keyval, keyval], axis=1)
    keyval = jnp.where(t < KV_HEADS, rope(doubled, tables), doubled).astype(BF16)
    out_kv[...] = keyval[:, :HEAD_DIM]
    kv_send[...] = keyval
    kind = t // KV_HEADS
    for j in range(2):
        target = (t % KV_HEADS) * 2 + j

        @pl.when(target != t)
        def _():
            pltpu.make_async_remote_copy(
                src_ref=kv_send, dst_ref=kv_recv.at[kind], send_sem=kv_ss.at[j],
                recv_sem=kv_rs.at[kind], device_id=(g, target), device_id_type=MESH,
            ).start()

        @pl.when(target == t)
        def _():
            kv_recv[kind] = kv_send[...]

    for d in range(1, 8):
        arrived(q_all.at[(t + 8 - d) % 8], z_recv.at[0, d])
    lane256 = lax.broadcasted_iota(jnp.int32, (REQ, KW), 1)
    pieces = []
    for h in range(HEADS):
        j, k = h % 4, h // 8
        slab = q_all[h // 4].astype(F32)
        shift = ((k - j) * HEAD_DIM) % KW
        if shift:
            slab = pltpu.roll(slab, shift, 1)
        pieces.append(jnp.where(lane256 // HEAD_DIM == k, slab, 0.0).astype(BF16))
    blocked = jnp.concatenate(pieces, axis=0)

    for d in (1, 3, 2):
        arrived(chunk((x + 4 - d) % 4, y, c), a_recv.at[0, d])
        part = half_chunk((x + 4 - d) % 4, y, c, 0)
        for e in (1, 3, 2):
            send(part, part, d_send.at[0, d, e], d_recv.at[0, d, e], y_peer[e])
        arrived(chunk(x, (y + 4 - d) % 4, c), a_recv.at[1, d])
        part = half_chunk(x, (y + 4 - d) % 4, c, 1)
        for e in (1, 3, 2):
            send(part, part, d_send.at[1, e, d], d_recv.at[1, e, d], x_peer[e])
    for d in (1, 3, 2):
        block = chunk((x + 4 - d) % 4, y, c)
        send(block, block, s_send.at[d, 0], s_recv.at[d, 0], sibling)
        block = chunk(x, (y + 4 - d) % 4, c)
        send(block, block, s_send.at[0, d], s_recv.at[0, d], sibling)

    lane3 = lax.broadcasted_iota(jnp.int32, (1, REQ, 128), 2)
    row3 = lax.broadcasted_iota(jnp.int32, (1, REQ, 128), 1)
    slot3 = lane3 % SLOTS + t * SLOTS
    own_half = lane3 // SLOTS == row3 % 2
    shape3 = (HEADS, REQ, 128)

    def pair_mask(pair, half):
        return (row3 // 2 == pair) & half

    def compact(key_quad, half, so_far):
        for q in range(4):
            wide = dot_t(blocked, key_quad(q))
            for e in range(2):
                block = wide[:, e * 128 : e * 128 + 128].reshape(shape3)
                so_far = jnp.where(pair_mask(q * 2 + e, half), block, so_far)
        return so_far

    def weigh(weights, value_quad, half):
        total = None
        for q in range(4):
            wide = jnp.concatenate(
                [
                    jnp.where(pair_mask(q * 2 + e, half), weights, 0.0).astype(BF16).reshape(ROWS, 128)
                    for e in range(2)
                ],
                axis=1,
            )
            term = dot(wide, value_quad(q))
            total = term if total is None else total + term
        return total

    def softmax_part(scores, valid):
        scores = jnp.where(valid, scores, LOW)
        maxima = jnp.max(scores, axis=-1, keepdims=True)
        weights = jnp.where(valid, jnp.exp(scores - maxima), 0.0)
        return weights, maxima, jnp.sum(weights, axis=-1, keepdims=True)

    locals_[4].wait()

    def own_rows(q, lanes):
        return v_priv[q * 4 : q * 4 + 4, :, lanes].reshape(4 * SLOTS, KW)

    keys, values = pl.ds(0, KW), pl.ds(KW, KW)
    scores = compact(lambda q: own_rows(q, keys), own_half, jnp.zeros(shape3, F32))
    valid = own_half & (slot3 < private_length.reshape(1, REQ, 128))
    weights, own_max, own_total = softmax_part(scores, valid)
    own_sum = weigh(weights, lambda q: own_rows(q, values), own_half)

    for d in (1, 3, 2):
        for e in (1, 3, 2):
            xx, yy = (x + 4 - d) % 4, (y + 4 - e) % 4
            arrived(half_chunk(xx, yy, c, 0), d_recv.at[0, d, e])
            arrived(half_chunk(xx, yy, c, 1), d_recv.at[1, d, e])
            block = chunk(xx, yy, c)
            send(block, block, s_send.at[d, e], s_recv.at[d, e], sibling)
    locals_[6].wait()
    for d in range(4):
        for e in range(4):
            arrived(chunk((x + 4 - d) % 4, (y + 4 - e) % 4, 1 - c), s_recv.at[d, e])

    def node_rows(q, lanes):
        order = (q * 4 + 1, q * 4, q * 4 + 3, q * 4 + 2)
        return jnp.concatenate([nodes[mids[r], :, lanes] for r in order], axis=0)

    root_keys = nodes[root, :, keys]
    root_values = nodes[root, :, values]
    root_scores = dot_t(blocked, jnp.concatenate([root_keys, root_keys], axis=0)).reshape(shape3)
    node_half = jnp.logical_not(own_half)
    scores = compact(lambda q: node_rows(q, keys), node_half, root_scores)
    limit = jnp.where(node_half, mid_length.reshape(1, REQ, 128), root_length)
    weights, tree_max, tree_total = softmax_part(scores, slot3 < limit)
    tree_sum = weigh(weights, lambda q: node_rows(q, values), node_half)
    tree_sum = tree_sum + dot(
        jnp.where(own_half, weights, 0.0).astype(BF16).reshape(ROWS, 128),
        jnp.concatenate([root_values, root_values], axis=0),
    )

    upper = jnp.maximum(own_max, tree_max)
    own_scale, tree_scale = jnp.exp(own_max - upper), jnp.exp(tree_max - upper)
    total = own_total * own_scale + tree_total * tree_scale
    narrow = []
    for k in range(KV_HEADS):
        rows, lanes = slice(128 * k, 128 * k + 128), slice(128 * (k // 2), 128 * (k // 2) + 128)
        piece = (
            own_sum[rows, lanes].reshape(8, REQ, 128) * own_scale[8 * k : 8 * k + 8]
            + tree_sum[rows, lanes].reshape(8, REQ, 128) * tree_scale[8 * k : 8 * k + 8]
        ).reshape(128, 128)
        narrow.append(pltpu.roll(piece, HEAD_DIM, 1) if k % 2 else piece)
    packed = jnp.concatenate(narrow, axis=0).reshape(shape3)
    for at, part in enumerate(three_parts(upper) + three_parts(total)):
        packed = jnp.where(lane3 == HEAD_DIM + at, part, packed)
    part_send[...] = packed.astype(BF16).reshape(8, 4 * REQ, 128)
    for d in (4, 3, 5, 2, 6, 1, 7):
        to = (t + d) % 8
        send(part_send.at[to], part_recv.at[t], z_send.at[1, d], z_recv.at[1, d], z_peer[d])

    @pl.when(t // 2 != t)
    def _():
        arrived(kv_recv.at[0], kv_rs.at[0])

    @pl.when(KV_HEADS + t // 2 != t)
    def _():
        arrived(kv_recv.at[1], kv_rs.at[1])

    queries = q_all[t].astype(F32)
    token_key = kv_recv[0].astype(F32)[:, :HEAD_DIM]
    token_value = kv_recv[1].astype(F32)[:, :HEAD_DIM]
    token_score = jnp.concatenate(
        [
            jnp.sum(queries[:, j * HEAD_DIM : (j + 1) * HEAD_DIM] * token_key, axis=-1, keepdims=True)
            for j in range(4)
        ],
        axis=0,
    )
    token_rows = jnp.concatenate([token_value] * 4, axis=0)

    part_recv[t] = part_send[t]
    for d in range(1, 8):
        arrived(part_recv.at[(t + 8 - d) % 8], z_recv.at[1, d])
    parts = [part_recv[s].astype(F32) for s in range(8)]

    def column(part, at):
        first = HEAD_DIM + at
        return part[:, first : first + 1] + part[:, first + 1 : first + 2] + part[:, first + 2 : first + 3]

    maxima = [column(part, 0) for part in parts]
    upper = token_score
    for entry in maxima:
        upper = jnp.maximum(upper, entry)
    fresh = jnp.exp(token_score - upper)
    total = fresh
    summed = fresh.astype(BF16).astype(F32) * token_rows
    for part, entry in zip(parts, maxima):
        factor = jnp.exp(entry - upper)
        total = total + column(part, 3) * factor
        summed = summed + part[:, :HEAD_DIM] * factor
    attention = (summed / total).astype(BF16)
    attention = jnp.concatenate([attention[j * REQ : (j + 1) * REQ] for j in range(4)], axis=1)

    locals_[5].wait()
    projected = dot(attention, v_wo[...])
    for s in range(8):
        rs_send[s] = projected[:, s * 256 : s * 256 + 256].astype(BF16)
    for d in (4, 3, 5, 2, 6, 1, 7):
        to = (t + d) % 8
        send(rs_send.at[to], rs_recv.at[t], z_send.at[2, d], z_recv.at[2, d], z_peer[d])
    rs_recv[t] = rs_send[t]
    for d in range(1, 8):
        arrived(rs_recv.at[(t + 8 - d) % 8], z_recv.at[2, d])
    result = v_hid[:, pl.ds(pl.multiple_of(t * 256, 256), 256)].astype(F32)
    for s in range(8):
        result = result + rs_recv[s].astype(F32)
    out_h[...] = result.astype(BF16)

    for copy in sends:
        copy.wait_send()
    for j in range(2):
        target = (t % KV_HEADS) * 2 + j

        @pl.when(target != t)
        def _():
            pltpu.make_async_copy(kv_send, kv_send, kv_ss.at[j]).wait()


def on_device(
    hidden_in, norm_gain, w_query, w_keyval, w_output, prefix_cache, private_cache,
    node_parent, node_length, request_node, private_length,
):
    anywhere = pl.BlockSpec(memory_space=pl.ANY)
    scalars = pl.BlockSpec(memory_space=pltpu.SMEM)
    vector = pl.BlockSpec(memory_space=pltpu.VMEM)
    dma = pltpu.SemaphoreType.DMA
    return pl.pallas_call(
        kernel,
        out_shape=(
            jax.ShapeDtypeStruct((REQ, 256), BF16),
            jax.ShapeDtypeStruct((REQ, HEAD_DIM), BF16),
        ),
        in_specs=[anywhere] * 7 + [scalars] * 4,
        out_specs=(vector, vector),
        scratch_shapes=[
            pltpu.VMEM((REQ, 2048), BF16),
            pltpu.VMEM((1, 2048), BF16),
            pltpu.VMEM((2048, 256), BF16),
            pltpu.VMEM((2048, 64), BF16),
            pltpu.VMEM((256, 2048), BF16),
            pltpu.VMEM((REQ, SLOTS, 512), BF16),
            pltpu.VMEM((64, SLOTS, 512), BF16),
            pltpu.VMEM((8, REQ, 256), BF16),
            pltpu.VMEM((REQ, 128), BF16),
            pltpu.VMEM((2, REQ, 128), BF16),
            pltpu.VMEM((8, 4 * REQ, 128), BF16),
            pltpu.VMEM((8, 4 * REQ, 128), BF16),
            pltpu.VMEM((8, REQ, 256), BF16),
            pltpu.VMEM((8, REQ, 256), BF16),
            dma((7,)),
            dma((2, 4)),
            dma((2, 4)),
            dma((2, 4, 4)),
            dma((2, 4, 4)),
            dma((4, 4)),
            dma((4, 4)),
            dma((3, 8)),
            dma((3, 8)),
            dma((2,)),
            dma((2,)),
        ],
        compiler_params=pltpu.CompilerParams(
            collective_id=0, has_side_effects=True, vmem_limit_bytes=48 * 1024 * 1024
        ),
    )(
        hidden_in, norm_gain.reshape(1, 2048), w_query, w_keyval, w_output, prefix_cache, private_cache,
        node_parent, node_length, request_node, private_length,
    )


def solution(mesh):
    placed = (
        P("grp", None), P(), P(None, "tp"), P(None, "tp"), P("tp", None), P("grp", "tp", None),
        P("grp", "tp", None), P(), P(), P(), P("grp"),
    )
    return jax.shard_map(
        on_device, mesh=mesh, in_specs=placed, out_specs=(P("grp", "tp"), P("grp", "tp")), check_vma=False
    )
```

```python
import math

import jax
import jax.numpy as jnp
from jax import lax
from jax.experimental import pallas as pl
from jax.experimental.pallas import tpu as pltpu
from jax.sharding import PartitionSpec as P

MESH = pl.DeviceIdType.MESH
F32 = jnp.float32
BF16 = jnp.bfloat16
HEADS = 32
KV_HEADS = 4
HEAD_DIM = 64
REQ = 16
SLOTS = 64
ROWS = HEADS * REQ
KW = KV_HEADS * HEAD_DIM
LOW = -1e30


def dot(a, b):
    return jnp.dot(a, b, preferred_element_type=F32)


def dot_t(a, b):
    return lax.dot_general(a, b, (((1,), (1,)), ((), ())), preferred_element_type=F32)


def three_parts(value):
    first = value.astype(BF16).astype(F32)
    rest = value - first
    second = rest.astype(BF16).astype(F32)
    third = (rest - second).astype(BF16).astype(F32)
    return first, second, third


def rope_tables(position):
    lane = lax.broadcasted_iota(jnp.int32, (REQ, 128), 1)
    index = (lane % (HEAD_DIM // 2)).astype(F32)
    frequency = jnp.exp(index * (-2.0 * math.log(10000.0) / HEAD_DIM))
    angle = position * frequency
    front = lane % HEAD_DIM < HEAD_DIM // 2
    sine = jnp.sin(angle)
    return jnp.cos(angle), jnp.where(front, -sine, sine), front


def rope(block, tables):
    cosine, sine, front = tables
    half = HEAD_DIM // 2
    swapped = jnp.where(front, pltpu.roll(block, 128 - half, 1), pltpu.roll(block, half, 1))
    return block * cosine + swapped * sine


def kernel(
    hid, gain, wq, wkv, wo, prefix, private, parent, nlen, reqnode, plen,
    out_h, out_kv,
    v_hid, v_gain, v_wq, v_wkv, v_wo, v_priv, nodes,
    q_all, kv_send, kv_recv, part_send, part_recv, rs_send, rs_recv,
    l_sem, d_send, d_recv, s_send, s_recv, z_send, z_recv, kv_ss, kv_rs,
):
    g = lax.axis_index("grp")
    t = lax.axis_index("tp")
    x, y, c = g // 8, (g // 2) % 4, g % 2

    def group(xx, yy, cc):
        return (xx * 4 + yy) * 2 + cc

    def chunk(xx, yy, cc):
        return nodes.at[pl.ds(group(xx, yy, cc) * 2, 2)]

    x_peer = {d: (group((x + 4 + d * (1 - 2 * c)) % 4, y, c), t) for d in (1, 2, -1)}
    y_peer = {d: (group(x, (y + 4 + d * (1 - 2 * c)) % 4, c), t) for d in (1, 2, -1)}
    sibling = (group(x, y, 1 - c), t)
    z_peer = [(g, (t + d) % 8) for d in range(8)]
    everyone = list(x_peer.values()) + list(y_peer.values()) + [sibling] + z_peer[1:]

    barrier = pltpu.get_barrier_semaphore()
    for peer in everyone:
        pl.semaphore_signal(barrier, inc=1, device_id=peer, device_id_type=MESH)

    locals_ = []
    for k, (src, dst) in enumerate(
        ((hid, v_hid), (gain, v_gain), (wq, v_wq), (wkv, v_wkv), (private, v_priv), (wo, v_wo),
         (prefix, chunk(x, y, c)))
    ):
        copy = pltpu.make_async_copy(src, dst, l_sem.at[k])
        copy.start()
        locals_.append(copy)

    def send(src, dst, ssem, rsem, peer):
        pltpu.make_async_remote_copy(
            src_ref=src, dst_ref=dst, send_sem=ssem, recv_sem=rsem, device_id=peer, device_id_type=MESH
        ).start()

    def arrived(ref, sem):
        pltpu.make_async_copy(ref, ref, sem).wait()

    turn = 1 - 2 * c

    def slab(i, a, b):
        return nodes.at[pl.ds(group((x + 16 - turn * a) % 4, (y + 16 - turn * b) % 4, c) * 2 + i, 1)]

    def hand_on(i, a, b, *ways):
        block = slab(i, a, b)
        for axis, step in ways:
            if axis == "s":
                send(block, block, s_send, s_recv, sibling)
                continue
            aa, bb = ((a + step) % 4, b) if axis == "x" else (a, (b + step) % 4)
            peer = (x_peer if axis == "x" else y_peer)[step]
            send(block, block, d_send, d_recv.at[i, aa, bb], peer)

    def relay(i, a, b, *ways):
        if i == 1:
            a, b = b, a
            ways = [({"x": "y", "y": "x"}[axis], step) for axis, step in ways]
        if a + b:
            arrived(slab(i, a, b), d_recv.at[i, a, b])
        hand_on(i, a, b, *ways, ("s", 0))

    mids = [reqnode[g * REQ + r] for r in range(REQ)]
    root = parent[mids[0]]
    root_length = nlen[root]
    row16 = lax.broadcasted_iota(jnp.int32, (REQ, 128), 0)
    lane16 = lax.broadcasted_iota(jnp.int32, (REQ, 128), 1)
    private_length = jnp.zeros((REQ, 128), jnp.int32)
    mid_length = jnp.zeros((REQ, 128), jnp.int32)
    for r in range(REQ):
        private_length = jnp.where(row16 == r, plen[r], private_length)
        mid_length = jnp.where(row16 == r, nlen[mids[r]], mid_length)
    tables = rope_tables((private_length + mid_length + root_length).astype(F32))

    locals_[0].wait()
    locals_[1].wait()
    floats = v_hid[...].astype(F32)
    spread = jnp.mean(floats * floats, axis=-1, keepdims=True)
    normed = (floats * lax.rsqrt(spread + 1e-05) * v_gain[...].reshape(1, 2048).astype(F32)).astype(BF16)
    locals_[2].wait()
    query = dot(normed, v_wq[...])
    for half in range(2):
        piece = rope(query[:, half * 128 : half * 128 + 128], tables).astype(BF16)
        q_all[t, :, half * 128 : half * 128 + 128] = piece * jnp.asarray(HEAD_DIM**-0.5, BF16)
    locals_[3].wait()
    keyval = dot_t(normed, v_wkv[...])
    doubled = jnp.concatenate([keyval, keyval], axis=1)
    keyval = jnp.where(t < KV_HEADS, rope(doubled, tables), doubled).astype(BF16)
    out_kv[...] = keyval[:, :HEAD_DIM]
    kv_send[...] = keyval
    locals_[6].wait()
    pl.semaphore_wait(barrier, len(everyone))
    hand_on(0, 0, 0, ("x", 2), ("x", 1), ("x", -1))
    hand_on(1, 0, 0, ("y", 2), ("y", 1), ("y", -1))
    for d in (4, 3, 5, 2, 6, 1, 7):
        send(q_all.at[t], q_all.at[t], z_send.at[0], z_recv.at[0], z_peer[d])
    hand_on(0, 0, 0, ("y", 1), ("y", -1), ("s", 0))
    hand_on(1, 0, 0, ("x", 1), ("x", -1), ("s", 0))

    kind = t // KV_HEADS
    for j in range(2):
        target = (t % KV_HEADS) * 2 + j

        @pl.when(target != t)
        def _():
            pltpu.make_async_remote_copy(
                src_ref=kv_send, dst_ref=kv_recv.at[kind], send_sem=kv_ss.at[j],
                recv_sem=kv_rs.at[kind], device_id=(g, target), device_id_type=MESH,
            ).start()

        @pl.when(target == t)
        def _():
            kv_recv[kind] = kv_send[...]

    def relay_first():
        for a in (1, 3):
            for i in range(2):
                relay(i, a, 0, ("y", 1), ("y", -1))
        for i in range(2):
            relay(i, 2, 0, ("y", 2), ("y", 1), ("y", -1))

    def relay_second():
        for i in range(2):
            relay(i, 0, 1, ("y", 1))
            relay(i, 0, 3)
        for i in range(2):
            relay(i, 1, 1, ("y", 1))
            relay(i, 3, 3, ("y", -1))

    def relay_last():
        for where in ((1, 3), (3, 1), (2, 1), (2, 3), (0, 2), (2, 2), (1, 2), (3, 2)):
            for i in range(2):
                relay(i, *where)
        arrived(nodes.at[pl.ds(0, 32)], s_recv)

    relay_first()

    arrived(q_all.at[pl.ds(0, 7)], z_recv.at[0])
    lane256 = lax.broadcasted_iota(jnp.int32, (REQ, KW), 1)
    pieces = []
    for h in range(HEADS):
        j, k = h % 4, h // 8
        four = q_all[h // 4].astype(F32)
        shift = ((k - j) * HEAD_DIM) % KW
        if shift:
            four = pltpu.roll(four, shift, 1)
        pieces.append(jnp.where(lane256 // HEAD_DIM == k, four, 0.0).astype(BF16))
    blocked = jnp.concatenate(pieces, axis=0)

    relay_second()
    lane3 = lax.broadcasted_iota(jnp.int32, (1, REQ, 128), 2)
    row3 = lax.broadcasted_iota(jnp.int32, (1, REQ, 128), 1)
    slot3 = lane3 % SLOTS + t * SLOTS
    own_half = lane3 // SLOTS == row3 % 2
    shape3 = (HEADS, REQ, 128)

    def pair_mask(pair, half):
        return (row3 // 2 == pair) & half

    def compact(key_quad, half, so_far):
        for q in range(4):
            wide = dot_t(blocked, key_quad(q))
            for e in range(2):
                block = wide[:, e * 128 : e * 128 + 128].reshape(shape3)
                so_far = jnp.where(pair_mask(q * 2 + e, half), block, so_far)
        return so_far

    def weigh(weights, value_quad, half):
        total = None
        for q in range(4):
            wide = jnp.concatenate(
                [
                    jnp.where(pair_mask(q * 2 + e, half), weights, 0.0).astype(BF16).reshape(ROWS, 128)
                    for e in range(2)
                ],
                axis=1,
            )
            term = dot(wide, value_quad(q))
            total = term if total is None else total + term
        return total

    def softmax_part(scores, valid):
        scores = jnp.where(valid, scores, LOW)
        maxima = jnp.max(scores, axis=-1, keepdims=True)
        weights = jnp.where(valid, jnp.exp(scores - maxima), 0.0)
        return weights, maxima, jnp.sum(weights, axis=-1, keepdims=True)

    locals_[4].wait()

    def own_rows(q, lanes):
        return v_priv[q * 4 : q * 4 + 4, :, lanes].reshape(4 * SLOTS, KW)

    keys, values = pl.ds(0, KW), pl.ds(KW, KW)
    scores = compact(lambda q: own_rows(q, keys), own_half, jnp.zeros(shape3, F32))
    valid = own_half & (slot3 < private_length.reshape(1, REQ, 128))
    weights, own_max, own_total = softmax_part(scores, valid)
    own_sum = weigh(weights, lambda q: own_rows(q, values), own_half)

    relay_last()

    def node_rows(q, lanes):
        order = (q * 4 + 1, q * 4, q * 4 + 3, q * 4 + 2)
        return jnp.concatenate([nodes[mids[r], :, lanes] for r in order], axis=0)

    root_keys = nodes[root, :, keys]
    root_values = nodes[root, :, values]
    root_scores = dot_t(blocked, jnp.concatenate([root_keys, root_keys], axis=0)).reshape(shape3)
    node_half = jnp.logical_not(own_half)
    scores = compact(lambda q: node_rows(q, keys), node_half, root_scores)
    limit = jnp.where(node_half, mid_length.reshape(1, REQ, 128), root_length)
    weights, tree_max, tree_total = softmax_part(scores, slot3 < limit)
    tree_sum = weigh(weights, lambda q: node_rows(q, values), node_half)
    tree_sum = tree_sum + dot(
        jnp.where(own_half, weights, 0.0).astype(BF16).reshape(ROWS, 128),
        jnp.concatenate([root_values, root_values], axis=0),
    )

    upper = jnp.maximum(own_max, tree_max)
    own_scale, tree_scale = jnp.exp(own_max - upper), jnp.exp(tree_max - upper)
    total = own_total * own_scale + tree_total * tree_scale
    narrow = []
    for k in range(KV_HEADS):
        rows, lanes = slice(128 * k, 128 * k + 128), slice(128 * (k // 2), 128 * (k // 2) + 128)
        piece = (
            own_sum[rows, lanes].reshape(8, REQ, 128) * own_scale[8 * k : 8 * k + 8]
            + tree_sum[rows, lanes].reshape(8, REQ, 128) * tree_scale[8 * k : 8 * k + 8]
        ).reshape(128, 128)
        narrow.append(pltpu.roll(piece, HEAD_DIM, 1) if k % 2 else piece)
    packed = jnp.concatenate(narrow, axis=0).reshape(shape3)
    for at, part in enumerate(three_parts(upper) + three_parts(total)):
        packed = jnp.where(lane3 == HEAD_DIM + at, part, packed)
    part_send[...] = packed.astype(BF16).reshape(8, 4 * REQ, 128)
    for d in (4, 3, 5, 2, 6, 1, 7):
        to = (t + d) % 8
        send(part_send.at[to], part_recv.at[t], z_send.at[1], z_recv.at[1], z_peer[d])

    arrived(nodes.at[pl.ds(0, 30)], d_send)
    arrived(nodes.at[pl.ds(0, 32)], s_send)
    arrived(q_all.at[pl.ds(0, 7)], z_send.at[0])
    @pl.when(t // 2 != t)
    def _():
        arrived(kv_recv.at[0], kv_rs.at[0])

    @pl.when(KV_HEADS + t // 2 != t)
    def _():
        arrived(kv_recv.at[1], kv_rs.at[1])

    queries = q_all[t].astype(F32)
    token_key = kv_recv[0].astype(F32)[:, :HEAD_DIM]
    token_value = kv_recv[1].astype(F32)[:, :HEAD_DIM]
    token_score = jnp.concatenate(
        [
            jnp.sum(queries[:, j * HEAD_DIM : (j + 1) * HEAD_DIM] * token_key, axis=-1, keepdims=True)
            for j in range(4)
        ],
        axis=0,
    )
    token_rows = jnp.concatenate([token_value] * 4, axis=0)

    part_recv[t] = part_send[t]
    arrived(part_recv.at[pl.ds(0, 7)], z_recv.at[1])
    parts = [part_recv[s].astype(F32) for s in range(8)]

    def column(part, at):
        first = HEAD_DIM + at
        return part[:, first : first + 1] + part[:, first + 1 : first + 2] + part[:, first + 2 : first + 3]

    maxima = [column(part, 0) for part in parts]
    upper = token_score
    for entry in maxima:
        upper = jnp.maximum(upper, entry)
    fresh = jnp.exp(token_score - upper)
    total = fresh
    summed = fresh.astype(BF16).astype(F32) * token_rows
    for part, entry in zip(parts, maxima):
        factor = jnp.exp(entry - upper)
        total = total + column(part, 3) * factor
        summed = summed + part[:, :HEAD_DIM] * factor
    attention = (summed / total).astype(BF16)
    attention = jnp.concatenate([attention[j * REQ : (j + 1) * REQ] for j in range(4)], axis=1)

    locals_[5].wait()
    for d in (4, 3, 5, 2, 6, 1, 7, 0):
        to = (t + d) % 8
        block = dot(attention, v_wo[:, pl.ds(pl.multiple_of(to * 256, 256), 256)]).astype(BF16)
        if d:
            rs_send[to] = block
            send(rs_send.at[to], rs_recv.at[t], z_send.at[2], z_recv.at[2], z_peer[d])
        else:
            rs_recv[t] = block
    arrived(rs_recv.at[pl.ds(0, 7)], z_recv.at[2])
    result = v_hid[:, pl.ds(pl.multiple_of(t * 256, 256), 256)].astype(F32)
    for s in range(8):
        result = result + rs_recv[s].astype(F32)
    out_h[...] = result.astype(BF16)

    arrived(part_send.at[pl.ds(0, 7)], z_send.at[1])
    arrived(rs_send.at[pl.ds(0, 7)], z_send.at[2])
    for j in range(2):
        target = (t % KV_HEADS) * 2 + j

        @pl.when(target != t)
        def _():
            pltpu.make_async_copy(kv_send, kv_send, kv_ss.at[j]).wait()


def on_device(
    hidden_in, norm_gain, w_query, w_keyval, w_output, prefix_cache, private_cache,
    node_parent, node_length, request_node, private_length,
):
    anywhere = pl.BlockSpec(memory_space=pltpu.HBM)
    scalars = pl.BlockSpec(memory_space=pltpu.SMEM)
    vector = pl.BlockSpec(memory_space=pltpu.VMEM)
    dma = pltpu.SemaphoreType.DMA
    return pl.pallas_call(
        kernel,
        out_shape=(
            jax.ShapeDtypeStruct((REQ, 256), BF16),
            jax.ShapeDtypeStruct((REQ, HEAD_DIM), BF16),
        ),
        in_specs=[anywhere] * 7 + [scalars] * 4,
        out_specs=(vector, vector),
        scratch_shapes=[
            pltpu.VMEM((REQ, 2048), BF16),
            pltpu.VMEM((2048,), BF16),
            pltpu.VMEM((2048, 256), BF16),
            pltpu.VMEM((64, 2048), BF16),
            pltpu.VMEM((256, 2048), BF16),
            pltpu.VMEM((REQ, SLOTS, 512), BF16),
            pltpu.VMEM((64, SLOTS, 512), BF16),
            pltpu.VMEM((8, REQ, 256), BF16),
            pltpu.VMEM((REQ, 128), BF16),
            pltpu.VMEM((2, REQ, 128), BF16),
            pltpu.VMEM((8, 4 * REQ, 128), BF16),
            pltpu.VMEM((8, 4 * REQ, 128), BF16),
            pltpu.VMEM((8, REQ, 256), BF16),
            pltpu.VMEM((8, REQ, 256), BF16),
            dma((7,)),
            dma,
            dma((2, 4, 4)),
            dma,
            dma,
            dma((3,)),
            dma((3,)),
            dma((2,)),
            dma((2,)),
        ],
        compiler_params=pltpu.CompilerParams(
            collective_id=0, has_side_effects=True, vmem_limit_bytes=63 * 1024 * 1024
        ),
    )(
        hidden_in, norm_gain, w_query, w_keyval.T, w_output, prefix_cache, private_cache,
        node_parent, node_length, request_node, private_length,
    )


def solution(mesh):
    placed = (
        P("grp", None), P(), P(None, "tp"), P(None, "tp"), P("tp", None), P("grp", "tp", None),
        P("grp", "tp", None), P(), P(), P(), P("grp"),
    )
    return jax.shard_map(
        on_device, mesh=mesh, in_specs=placed, out_specs=(P("grp", "tp"), P("grp", "tp")), check_vma=False
    )
```

```python
import math

import jax
import jax.numpy as jnp
from jax import lax
from jax.experimental import pallas as pl
from jax.experimental.pallas import tpu as pltpu
from jax.sharding import PartitionSpec as P

MESH = pl.DeviceIdType.MESH
F32 = jnp.float32
BF16 = jnp.bfloat16
HEADS = 32
KV_HEADS = 4
HEAD_DIM = 64
REQ = 16
SLOTS = 64
ROWS = HEADS * REQ
KW = KV_HEADS * HEAD_DIM
LOW = -1e30


def dot(a, b):
    return jnp.dot(a, b, preferred_element_type=F32)


def dot_t(a, b):
    return lax.dot_general(a, b, (((1,), (1,)), ((), ())), preferred_element_type=F32)


def three_parts(value):
    first = value.astype(BF16).astype(F32)
    rest = value - first
    second = rest.astype(BF16).astype(F32)
    third = (rest - second).astype(BF16).astype(F32)
    return first, second, third


def rope_tables(position):
    lane = lax.broadcasted_iota(jnp.int32, (REQ, 128), 1)
    index = (lane % (HEAD_DIM // 2)).astype(F32)
    frequency = jnp.exp(index * (-2.0 * math.log(10000.0) / HEAD_DIM))
    angle = position * frequency
    front = lane % HEAD_DIM < HEAD_DIM // 2
    sine = jnp.sin(angle)
    return jnp.cos(angle), jnp.where(front, -sine, sine), front


def rope(block, tables):
    cosine, sine, front = tables
    half = HEAD_DIM // 2
    swapped = jnp.where(front, pltpu.roll(block, 128 - half, 1), pltpu.roll(block, half, 1))
    return block * cosine + swapped * sine


def kernel(
    hid, gain, wq, wkv, wo, prefix, private, parent, nlen, reqnode, plen,
    out_h, out_kv,
    v_hid, v_gain, v_wq, v_wkv, v_wo, v_priv, nodes,
    q_all, kv_send, kv_recv, part_send, part_recv, rs_send, rs_recv,
    l_sem, d_send, d_recv, s_send, s_recv, z_send, z_recv, kv_ss, kv_rs,
):
    g = lax.axis_index("grp")
    t = lax.axis_index("tp")
    x, y, c = g // 8, (g // 2) % 4, g % 2

    def group(xx, yy, cc):
        return (xx * 4 + yy) * 2 + cc

    def chunk(xx, yy, cc):
        return nodes.at[pl.ds(group(xx, yy, cc) * 2, 2)]

    x_peer = {d: (group((x + 4 + d * (1 - 2 * c)) % 4, y, c), t) for d in (1, 2, -1)}
    y_peer = {d: (group(x, (y + 4 + d * (1 - 2 * c)) % 4, c), t) for d in (1, 2, -1)}
    sibling = (group(x, y, 1 - c), t)
    z_peer = [(g, (t + d) % 8) for d in range(8)]
    everyone = list(x_peer.values()) + list(y_peer.values()) + [sibling] + z_peer[1:]

    barrier = pltpu.get_barrier_semaphore()
    for peer in everyone:
        pl.semaphore_signal(barrier, inc=1, device_id=peer, device_id_type=MESH)

    locals_ = []
    for k, (src, dst) in enumerate(
        ((hid, v_hid), (gain, v_gain), (wq, v_wq), (wkv, v_wkv), (private, v_priv), (wo, v_wo),
         (prefix, chunk(x, y, c)))
    ):
        copy = pltpu.make_async_copy(src, dst, l_sem.at[k])
        copy.start()
        locals_.append(copy)

    def send(src, dst, ssem, rsem, peer):
        pltpu.make_async_remote_copy(
            src_ref=src, dst_ref=dst, send_sem=ssem, recv_sem=rsem, device_id=peer, device_id_type=MESH
        ).start()

    def arrived(ref, sem):
        pltpu.make_async_copy(ref, ref, sem).wait()

    turn = 1 - 2 * c

    def slab(i, a, b):
        return nodes.at[pl.ds(group((x + 16 - turn * a) % 4, (y + 16 - turn * b) % 4, c) * 2 + i, 1)]

    def hand_on(i, a, b, *ways):
        block = prefix.at[pl.ds(i, 1)] if a + b == 0 else slab(i, a, b)
        for axis, step in ways:
            if axis == "s":
                send(block, slab(i, a, b), s_send, s_recv, sibling)
                continue
            aa, bb = ((a + step) % 4, b) if axis == "x" else (a, (b + step) % 4)
            peer = (x_peer if axis == "x" else y_peer)[step]
            send(block, slab(i, a, b), d_send, d_recv.at[i, aa, bb], peer)

    def relay(i, a, b, *ways):
        if i == 1:
            a, b = b, a
            ways = [({"x": "y", "y": "x"}[axis], step) for axis, step in ways]
        if a + b:
            arrived(slab(i, a, b), d_recv.at[i, a, b])
        hand_on(i, a, b, *ways, ("s", 0))

    pl.semaphore_wait(barrier, len(everyone))
    hand_on(0, 0, 0, ("x", 2), ("x", 1), ("x", -1))
    hand_on(1, 0, 0, ("y", 2), ("y", 1), ("y", -1))
    hand_on(0, 0, 0, ("y", 1), ("y", -1), ("s", 0))
    hand_on(1, 0, 0, ("x", 1), ("x", -1), ("s", 0))

    mids = [reqnode[g * REQ + r] for r in range(REQ)]
    root = parent[mids[0]]
    root_length = nlen[root]
    row16 = lax.broadcasted_iota(jnp.int32, (REQ, 128), 0)
    lane16 = lax.broadcasted_iota(jnp.int32, (REQ, 128), 1)
    private_length = jnp.zeros((REQ, 128), jnp.int32)
    mid_length = jnp.zeros((REQ, 128), jnp.int32)
    for r in range(REQ):
        private_length = jnp.where(row16 == r, plen[r], private_length)
        mid_length = jnp.where(row16 == r, nlen[mids[r]], mid_length)
    tables = rope_tables((private_length + mid_length + root_length).astype(F32))

    locals_[0].wait()
    locals_[1].wait()
    floats = v_hid[...].astype(F32)
    spread = jnp.mean(floats * floats, axis=-1, keepdims=True)
    normed = (floats * lax.rsqrt(spread + 1e-05) * v_gain[...].reshape(1, 2048).astype(F32)).astype(BF16)
    locals_[2].wait()
    query = dot(normed, v_wq[...])
    for half in range(2):
        piece = rope(query[:, half * 128 : half * 128 + 128], tables).astype(BF16)
        q_all[t, :, half * 128 : half * 128 + 128] = piece * jnp.asarray(HEAD_DIM**-0.5, BF16)
    locals_[3].wait()
    keyval = dot_t(normed, v_wkv[...])
    doubled = jnp.concatenate([keyval, keyval], axis=1)
    keyval = jnp.where(t < KV_HEADS, rope(doubled, tables), doubled).astype(BF16)
    out_kv[...] = keyval[:, :HEAD_DIM]
    kv_send[...] = keyval
    for d in (4, 3, 5, 2, 6, 1, 7):
        send(q_all.at[t], q_all.at[t], z_send.at[0], z_recv.at[0], z_peer[d])
    kind = t // KV_HEADS
    for j in range(2):
        target = (t % KV_HEADS) * 2 + j

        @pl.when(target != t)
        def _():
            pltpu.make_async_remote_copy(
                src_ref=kv_send, dst_ref=kv_recv.at[kind], send_sem=kv_ss.at[j],
                recv_sem=kv_rs.at[kind], device_id=(g, target), device_id_type=MESH,
            ).start()

        @pl.when(target == t)
        def _():
            kv_recv[kind] = kv_send[...]

    def relay_first():
        for a in (1, 3):
            for i in range(2):
                relay(i, a, 0, ("y", 1), ("y", -1))
        for i in range(2):
            relay(i, 2, 0, ("y", 2), ("y", 1), ("y", -1))

    def relay_second():
        for i in range(2):
            relay(i, 0, 1, ("y", 1))
            relay(i, 0, 3)
        for i in range(2):
            relay(i, 1, 1, ("y", 1))
            relay(i, 3, 3, ("y", -1))

    def relay_last():
        for where in ((1, 3), (3, 1), (2, 1), (2, 3), (0, 2), (2, 2), (1, 2), (3, 2)):
            for i in range(2):
                relay(i, *where)
        arrived(nodes.at[pl.ds(0, 32)], s_recv)

    relay_first()

    arrived(q_all.at[pl.ds(0, 7)], z_recv.at[0])
    lane256 = lax.broadcasted_iota(jnp.int32, (REQ, KW), 1)
    pieces = []
    for h in range(HEADS):
        j, k = h % 4, h // 8
        four = q_all[h // 4].astype(F32)
        shift = ((k - j) * HEAD_DIM) % KW
        if shift:
            four = pltpu.roll(four, shift, 1)
        pieces.append(jnp.where(lane256 // HEAD_DIM == k, four, 0.0).astype(BF16))
    blocked = jnp.concatenate(pieces, axis=0)

    relay_second()
    lane3 = lax.broadcasted_iota(jnp.int32, (1, REQ, 128), 2)
    row3 = lax.broadcasted_iota(jnp.int32, (1, REQ, 128), 1)
    slot3 = lane3 % SLOTS + t * SLOTS
    own_half = lane3 // SLOTS == row3 % 2
    shape3 = (HEADS, REQ, 128)

    def pair_mask(pair, half):
        return (row3 // 2 == pair) & half

    def compact(key_quad, half, so_far):
        for q in range(4):
            wide = dot_t(blocked, key_quad(q))
            for e in range(2):
                block = wide[:, e * 128 : e * 128 + 128].reshape(shape3)
                so_far = jnp.where(pair_mask(q * 2 + e, half), block, so_far)
        return so_far

    def weigh(weights, value_quad, half):
        total = None
        for q in range(4):
            wide = jnp.concatenate(
                [
                    jnp.where(pair_mask(q * 2 + e, half), weights, 0.0).astype(BF16).reshape(ROWS, 128)
                    for e in range(2)
                ],
                axis=1,
            )
            term = dot(wide, value_quad(q))
            total = term if total is None else total + term
        return total

    def softmax_part(scores, valid):
        scores = jnp.where(valid, scores, LOW)
        maxima = jnp.max(scores, axis=-1, keepdims=True)
        weights = jnp.where(valid, jnp.exp(scores - maxima), 0.0)
        return weights, maxima, jnp.sum(weights, axis=-1, keepdims=True)

    locals_[4].wait()

    def own_rows(q, lanes):
        return v_priv[q * 4 : q * 4 + 4, :, lanes].reshape(4 * SLOTS, KW)

    keys, values = pl.ds(0, KW), pl.ds(KW, KW)
    scores = compact(lambda q: own_rows(q, keys), own_half, jnp.zeros(shape3, F32))
    valid = own_half & (slot3 < private_length.reshape(1, REQ, 128))
    weights, own_max, own_total = softmax_part(scores, valid)
    own_sum = weigh(weights, lambda q: own_rows(q, values), own_half)

    relay_last()
    locals_[6].wait()

    def node_rows(q, lanes):
        order = (q * 4 + 1, q * 4, q * 4 + 3, q * 4 + 2)
        return jnp.concatenate([nodes[mids[r], :, lanes] for r in order], axis=0)

    root_keys = nodes[root, :, keys]
    root_values = nodes[root, :, values]
    root_scores = dot_t(blocked, jnp.concatenate([root_keys, root_keys], axis=0)).reshape(shape3)
    node_half = jnp.logical_not(own_half)
    scores = compact(lambda q: node_rows(q, keys), node_half, root_scores)
    limit = jnp.where(node_half, mid_length.reshape(1, REQ, 128), root_length)
    weights, tree_max, tree_total = softmax_part(scores, slot3 < limit)
    tree_sum = weigh(weights, lambda q: node_rows(q, values), node_half)
    tree_sum = tree_sum + dot(
        jnp.where(own_half, weights, 0.0).astype(BF16).reshape(ROWS, 128),
        jnp.concatenate([root_values, root_values], axis=0),
    )

    upper = jnp.maximum(own_max, tree_max)
    own_scale, tree_scale = jnp.exp(own_max - upper), jnp.exp(tree_max - upper)
    total = own_total * own_scale + tree_total * tree_scale
    narrow = []
    for k in range(KV_HEADS):
        rows, lanes = slice(128 * k, 128 * k + 128), slice(128 * (k // 2), 128 * (k // 2) + 128)
        piece = (
            own_sum[rows, lanes].reshape(8, REQ, 128) * own_scale[8 * k : 8 * k + 8]
            + tree_sum[rows, lanes].reshape(8, REQ, 128) * tree_scale[8 * k : 8 * k + 8]
        ).reshape(128, 128)
        narrow.append(pltpu.roll(piece, HEAD_DIM, 1) if k % 2 else piece)
    packed = jnp.concatenate(narrow, axis=0).reshape(shape3)
    for at, part in enumerate(three_parts(upper) + three_parts(total)):
        packed = jnp.where(lane3 == HEAD_DIM + at, part, packed)
    part_send[...] = packed.astype(BF16).reshape(8, 4 * REQ, 128)
    for d in (4, 3, 5, 2, 6, 1, 7):
        to = (t + d) % 8
        send(part_send.at[to], part_recv.at[t], z_send.at[1], z_recv.at[1], z_peer[d])

    arrived(nodes.at[pl.ds(0, 30)], d_send)
    arrived(nodes.at[pl.ds(0, 32)], s_send)
    arrived(q_all.at[pl.ds(0, 7)], z_send.at[0])
    @pl.when(t // 2 != t)
    def _():
        arrived(kv_recv.at[0], kv_rs.at[0])

    @pl.when(KV_HEADS + t // 2 != t)
    def _():
        arrived(kv_recv.at[1], kv_rs.at[1])

    queries = q_all[t].astype(F32)
    token_key = kv_recv[0].astype(F32)[:, :HEAD_DIM]
    token_value = kv_recv[1].astype(F32)[:, :HEAD_DIM]
    token_score = jnp.concatenate(
        [
            jnp.sum(queries[:, j * HEAD_DIM : (j + 1) * HEAD_DIM] * token_key, axis=-1, keepdims=True)
            for j in range(4)
        ],
        axis=0,
    )
    token_rows = jnp.concatenate([token_value] * 4, axis=0)

    part_recv[t] = part_send[t]
    arrived(part_recv.at[pl.ds(0, 7)], z_recv.at[1])
    parts = [part_recv[s].astype(F32) for s in range(8)]

    def column(part, at):
        first = HEAD_DIM + at
        return part[:, first : first + 1] + part[:, first + 1 : first + 2] + part[:, first + 2 : first + 3]

    maxima = [column(part, 0) for part in parts]
    upper = token_score
    for entry in maxima:
        upper = jnp.maximum(upper, entry)
    fresh = jnp.exp(token_score - upper)
    total = fresh
    summed = fresh.astype(BF16).astype(F32) * token_rows
    for part, entry in zip(parts, maxima):
        factor = jnp.exp(entry - upper)
        total = total + column(part, 3) * factor
        summed = summed + part[:, :HEAD_DIM] * factor
    attention = (summed / total).astype(BF16)
    attention = jnp.concatenate([attention[j * REQ : (j + 1) * REQ] for j in range(4)], axis=1)

    locals_[5].wait()
    for d in (4, 3, 5, 2, 6, 1, 7, 0):
        to = (t + d) % 8
        block = dot(attention, v_wo[:, pl.ds(pl.multiple_of(to * 256, 256), 256)]).astype(BF16)
        if d:
            rs_send[to] = block
            send(rs_send.at[to], rs_recv.at[t], z_send.at[2], z_recv.at[2], z_peer[d])
        else:
            rs_recv[t] = block
    arrived(rs_recv.at[pl.ds(0, 7)], z_recv.at[2])
    result = v_hid[:, pl.ds(pl.multiple_of(t * 256, 256), 256)].astype(F32)
    for s in range(8):
        result = result + rs_recv[s].astype(F32)
    out_h[...] = result.astype(BF16)

    arrived(part_send.at[pl.ds(0, 7)], z_send.at[1])
    arrived(rs_send.at[pl.ds(0, 7)], z_send.at[2])
    for j in range(2):
        target = (t % KV_HEADS) * 2 + j

        @pl.when(target != t)
        def _():
            pltpu.make_async_copy(kv_send, kv_send, kv_ss.at[j]).wait()


def on_device(
    hidden_in, norm_gain, w_query, w_keyval, w_output, prefix_cache, private_cache,
    node_parent, node_length, request_node, private_length,
):
    anywhere = pl.BlockSpec(memory_space=pltpu.HBM)
    scalars = pl.BlockSpec(memory_space=pltpu.SMEM)
    vector = pl.BlockSpec(memory_space=pltpu.VMEM)
    dma = pltpu.SemaphoreType.DMA
    return pl.pallas_call(
        kernel,
        out_shape=(
            jax.ShapeDtypeStruct((REQ, 256), BF16),
            jax.ShapeDtypeStruct((REQ, HEAD_DIM), BF16),
        ),
        in_specs=[anywhere] * 7 + [scalars] * 4,
        out_specs=(vector, vector),
        scratch_shapes=[
            pltpu.VMEM((REQ, 2048), BF16),
            pltpu.VMEM((2048,), BF16),
            pltpu.VMEM((2048, 256), BF16),
            pltpu.VMEM((64, 2048), BF16),
            pltpu.VMEM((256, 2048), BF16),
            pltpu.VMEM((REQ, SLOTS, 512), BF16),
            pltpu.VMEM((64, SLOTS, 512), BF16),
            pltpu.VMEM((8, REQ, 256), BF16),
            pltpu.VMEM((REQ, 128), BF16),
            pltpu.VMEM((2, REQ, 128), BF16),
            pltpu.VMEM((8, 4 * REQ, 128), BF16),
            pltpu.VMEM((8, 4 * REQ, 128), BF16),
            pltpu.VMEM((8, REQ, 256), BF16),
            pltpu.VMEM((8, REQ, 256), BF16),
            dma((7,)),
            dma,
            dma((2, 4, 4)),
            dma,
            dma,
            dma((3,)),
            dma((3,)),
            dma((2,)),
            dma((2,)),
        ],
        compiler_params=pltpu.CompilerParams(
            collective_id=0, has_side_effects=True, vmem_limit_bytes=40 * 1024 * 1024
        ),
    )(
        *(
            pltpu.with_memory_space_constraint(array, pltpu.HBM)
            for array in (
                hidden_in, norm_gain, w_query, w_keyval.T, w_output, prefix_cache, private_cache,
                node_parent, node_length, request_node, private_length,
            )
        )
    )


def solution(mesh):
    placed = (
        P("grp", None), P(), P(None, "tp"), P(None, "tp"), P("tp", None), P("grp", "tp", None),
        P("grp", "tp", None), P(), P(), P(), P("grp"),
    )
    return jax.shard_map(
        on_device, mesh=mesh, in_specs=placed, out_specs=(P("grp", "tp"), P("grp", "tp")), check_vma=False
    )
```

```python
import math

import jax
import jax.numpy as jnp
from jax import lax
from jax.experimental import pallas as pl
from jax.experimental.pallas import tpu as pltpu
from jax.sharding import PartitionSpec as P

MESH = pl.DeviceIdType.MESH
F32 = jnp.float32
BF16 = jnp.bfloat16
HEADS = 32
KV_HEADS = 4
HEAD_DIM = 64
REQ = 16
SLOTS = 64
ROWS = HEADS * REQ
KW = KV_HEADS * HEAD_DIM
LOW = -1e30


def dot(a, b):
    return jnp.dot(a, b, preferred_element_type=F32)


def dot_t(a, b):
    return lax.dot_general(a, b, (((1,), (1,)), ((), ())), preferred_element_type=F32)


def three_parts(value):
    first = value.astype(BF16).astype(F32)
    rest = value - first
    second = rest.astype(BF16).astype(F32)
    third = (rest - second).astype(BF16).astype(F32)
    return first, second, third


def rope_tables(position):
    lane = lax.broadcasted_iota(jnp.int32, (REQ, 128), 1)
    index = (lane % (HEAD_DIM // 2)).astype(F32)
    frequency = jnp.exp(index * (-2.0 * math.log(10000.0) / HEAD_DIM))
    angle = position * frequency
    front = lane % HEAD_DIM < HEAD_DIM // 2
    sine = jnp.sin(angle)
    return jnp.cos(angle), jnp.where(front, -sine, sine), front


def rope(block, tables):
    cosine, sine, front = tables
    half = HEAD_DIM // 2
    swapped = jnp.where(front, pltpu.roll(block, 128 - half, 1), pltpu.roll(block, half, 1))
    return block * cosine + swapped * sine


def kernel(
    hid, gain, wq, wkv, wo, prefix, private, parent, nlen, reqnode, plen,
    out_h, out_kv,
    v_hid, v_gain, v_wq, v_wkv, v_wo, v_priv, nodes,
    q_all, kv_send, kv_recv, part_send, part_recv, rs_send, rs_recv,
    l_sem, d_send, d_recv, s_send, s_recv, z_send, z_recv, kv_ss, kv_rs,
):
    g = lax.axis_index("grp")
    t = lax.axis_index("tp")
    x, y, c = g // 8, (g // 2) % 4, g % 2

    def group(xx, yy, cc):
        return (xx * 4 + yy) * 2 + cc

    def chunk(xx, yy, cc):
        return nodes.at[pl.ds(group(xx, yy, cc) * 2, 2)]

    x_peer = {d: (group((x + 4 + d * (1 - 2 * c)) % 4, y, c), t) for d in (1, 2, -1)}
    y_peer = {d: (group(x, (y + 4 + d * (1 - 2 * c)) % 4, c), t) for d in (1, 2, -1)}
    sibling = (group(x, y, 1 - c), t)
    z_peer = [(g, (t + d) % 8) for d in range(8)]
    everyone = list(x_peer.values()) + list(y_peer.values()) + [sibling] + z_peer[1:]

    barrier = pltpu.get_barrier_semaphore()
    for peer in everyone:
        pl.semaphore_signal(barrier, inc=1, device_id=peer, device_id_type=MESH)

    locals_ = []
    for k, (src, dst) in enumerate(
        ((hid, v_hid), (gain, v_gain), (wq, v_wq), (wkv, v_wkv), (private, v_priv), (wo, v_wo),
         (prefix, chunk(x, y, c)))
    ):
        copy = pltpu.make_async_copy(src, dst, l_sem.at[k])
        copy.start()
        locals_.append(copy)

    def send(src, dst, ssem, rsem, peer):
        pltpu.make_async_remote_copy(
            src_ref=src, dst_ref=dst, send_sem=ssem, recv_sem=rsem, device_id=peer, device_id_type=MESH
        ).start()

    def arrived(ref, sem):
        pltpu.make_async_copy(ref, ref, sem).wait()

    turn = 1 - 2 * c

    def slab(i, a, b):
        return nodes.at[pl.ds(group((x + 16 - turn * a) % 4, (y + 16 - turn * b) % 4, c) * 2 + i, 1)]

    def hand_on(i, a, b, *ways):
        block = prefix.at[pl.ds(i, 1)] if a + b == 0 else slab(i, a, b)
        for axis, step in ways:
            if axis == "s":
                send(block, slab(i, a, b), s_send, s_recv, sibling)
                continue
            aa, bb = ((a + step) % 4, b) if axis == "x" else (a, (b + step) % 4)
            peer = (x_peer if axis == "x" else y_peer)[step]
            send(block, slab(i, a, b), d_send, d_recv.at[i, aa, bb], peer)

    def relay(i, a, b, *ways):
        if i == 1:
            a, b = b, a
            ways = [({"x": "y", "y": "x"}[axis], step) for axis, step in ways]
        if a + b:
            arrived(slab(i, a, b), d_recv.at[i, a, b])
        hand_on(i, a, b, *ways, ("s", 0))

    pl.semaphore_wait(barrier, len(everyone))
    hand_on(0, 0, 0, ("x", 2), ("x", 1), ("x", -1))
    hand_on(1, 0, 0, ("y", 2), ("y", 1), ("y", -1))
    hand_on(0, 0, 0, ("y", 1), ("y", -1), ("s", 0))
    hand_on(1, 0, 0, ("x", 1), ("x", -1), ("s", 0))

    mids = [reqnode[g * REQ + r] for r in range(REQ)]
    root = parent[mids[0]]
    root_length = nlen[root]
    row16 = lax.broadcasted_iota(jnp.int32, (REQ, 128), 0)
    lane16 = lax.broadcasted_iota(jnp.int32, (REQ, 128), 1)
    private_length = jnp.zeros((REQ, 128), jnp.int32)
    mid_length = jnp.zeros((REQ, 128), jnp.int32)
    for r in range(REQ):
        private_length = jnp.where(row16 == r, plen[r], private_length)
        mid_length = jnp.where(row16 == r, nlen[mids[r]], mid_length)
    tables = rope_tables((private_length + mid_length + root_length).astype(F32))

    locals_[0].wait()
    locals_[1].wait()
    floats = v_hid[...].astype(F32)
    spread = jnp.mean(floats * floats, axis=-1, keepdims=True)
    normed = (floats * lax.rsqrt(spread + 1e-05) * v_gain[...].reshape(1, 2048).astype(F32)).astype(BF16)
    locals_[2].wait()
    query = dot(normed, v_wq[...])
    for half in range(2):
        piece = rope(query[:, half * 128 : half * 128 + 128], tables).astype(BF16)
        q_all[t, :, half * 128 : half * 128 + 128] = piece * jnp.asarray(HEAD_DIM**-0.5, BF16)
    locals_[3].wait()
    keyval = dot_t(normed, v_wkv[...])
    doubled = jnp.concatenate([keyval, keyval], axis=1)
    keyval = jnp.where(t < KV_HEADS, rope(doubled, tables), doubled).astype(BF16)
    out_kv[...] = keyval[:, :HEAD_DIM]
    kv_send[...] = keyval
    for d in (4, 3, 5, 2, 6, 1, 7):
        send(q_all.at[t], q_all.at[t], z_send.at[0], z_recv.at[0], z_peer[d])
    kind = t // KV_HEADS
    for j in range(2):
        target = (t % KV_HEADS) * 2 + j

        @pl.when(target != t)
        def _():
            pltpu.make_async_remote_copy(
                src_ref=kv_send, dst_ref=kv_recv.at[kind], send_sem=kv_ss.at[j],
                recv_sem=kv_rs.at[kind], device_id=(g, target), device_id_type=MESH,
            ).start()

        @pl.when(target == t)
        def _():
            kv_recv[kind] = kv_send[...]

    def relay_first():
        for a in (1, 3):
            for i in range(2):
                relay(i, a, 0, ("y", 1), ("y", -1))
        for i in range(2):
            relay(i, 2, 0, ("y", 2), ("y", 1), ("y", -1))

    def relay_second():
        for i in range(2):
            relay(i, 0, 1, ("y", 1))
            relay(i, 0, 3)
        for i in range(2):
            relay(i, 1, 1, ("y", 1))
            relay(i, 3, 3, ("y", -1))

    def relay_last():
        for where in ((1, 3), (3, 1), (2, 1), (2, 3), (0, 2), (2, 2), (1, 2), (3, 2)):
            for i in range(2):
                relay(i, *where)
        arrived(nodes.at[pl.ds(0, 32)], s_recv)

    relay_first()

    arrived(q_all.at[pl.ds(0, 7)], z_recv.at[0])
    lane256 = lax.broadcasted_iota(jnp.int32, (REQ, KW), 1)
    pieces = []
    for h in range(HEADS):
        j, k = h % 4, h // 8
        four = q_all[h // 4].astype(F32)
        shift = ((k - j) * HEAD_DIM) % KW
        if shift:
            four = pltpu.roll(four, shift, 1)
        pieces.append(jnp.where(lane256 // HEAD_DIM == k, four, 0.0).astype(BF16))
    blocked = jnp.concatenate(pieces, axis=0)

    relay_second()
    lane3 = lax.broadcasted_iota(jnp.int32, (1, REQ, 128), 2)
    row3 = lax.broadcasted_iota(jnp.int32, (1, REQ, 128), 1)
    slot3 = lane3 % SLOTS + t * SLOTS
    own_half = lane3 // SLOTS == row3 % 2
    shape3 = (HEADS, REQ, 128)

    def pair_mask(pair, half):
        return (row3 // 2 == pair) & half

    def compact(key_quad, half, so_far):
        for q in range(4):
            wide = dot_t(blocked, key_quad(q))
            for e in range(2):
                block = wide[:, e * 128 : e * 128 + 128].reshape(shape3)
                so_far = jnp.where(pair_mask(q * 2 + e, half), block, so_far)
        return so_far

    def weigh(weights, value_quad, half):
        total = None
        for q in range(4):
            wide = jnp.concatenate(
                [
                    jnp.where(pair_mask(q * 2 + e, half), weights, 0.0).astype(BF16).reshape(ROWS, 128)
                    for e in range(2)
                ],
                axis=1,
            )
            term = dot(wide, value_quad(q))
            total = term if total is None else total + term
        return total

    def softmax_part(scores, valid):
        scores = jnp.where(valid, scores, LOW)
        maxima = jnp.max(scores, axis=-1, keepdims=True)
        weights = jnp.where(valid, jnp.exp(scores - maxima), 0.0)
        return weights, maxima, jnp.sum(weights, axis=-1, keepdims=True)

    locals_[4].wait()

    def own_rows(q, lanes):
        return v_priv[q * 4 : q * 4 + 4, :, lanes].reshape(4 * SLOTS, KW)

    keys, values = pl.ds(0, KW), pl.ds(KW, KW)
    scores = compact(lambda q: own_rows(q, keys), own_half, jnp.zeros(shape3, F32))
    valid = own_half & (slot3 < private_length.reshape(1, REQ, 128))
    weights, own_max, own_total = softmax_part(scores, valid)
    own_sum = weigh(weights, lambda q: own_rows(q, values), own_half)

    relay_last()
    locals_[6].wait()

    def node_rows(q, lanes):
        order = (q * 4 + 1, q * 4, q * 4 + 3, q * 4 + 2)
        return jnp.concatenate([nodes[mids[r], :, lanes] for r in order], axis=0)

    root_keys = nodes[root, :, keys]
    root_values = nodes[root, :, values]
    root_scores = dot_t(blocked, jnp.concatenate([root_keys, root_keys], axis=0)).reshape(shape3)
    node_half = jnp.logical_not(own_half)
    scores = compact(lambda q: node_rows(q, keys), node_half, root_scores)
    limit = jnp.where(node_half, mid_length.reshape(1, REQ, 128), root_length)
    weights, tree_max, tree_total = softmax_part(scores, slot3 < limit)
    tree_sum = weigh(weights, lambda q: node_rows(q, values), node_half)
    tree_sum = tree_sum + dot(
        jnp.where(own_half, weights, 0.0).astype(BF16).reshape(ROWS, 128),
        jnp.concatenate([root_values, root_values], axis=0),
    )

    upper = jnp.maximum(own_max, tree_max)
    own_scale, tree_scale = jnp.exp(own_max - upper), jnp.exp(tree_max - upper)
    total = own_total * own_scale + tree_total * tree_scale
    stats = three_parts(upper) + three_parts(total)
    low_half = lane16 < HEAD_DIM
    for p in range(8):
        for b in range(2):
            pair = []
            for e in range(2):
                h = 4 * p + 2 * b + e
                k = h // 8
                rows, lanes = slice(REQ * h, REQ * h + REQ), slice(128 * (k // 2), 128 * (k // 2) + 128)
                piece = own_sum[rows, lanes] * own_scale[h] + tree_sum[rows, lanes] * tree_scale[h]
                pair.append(piece if k % 2 == e else pltpu.roll(piece, HEAD_DIM, 1))
            part_send[p, :, 128 * b : 128 * b + 128] = jnp.where(low_half, *pair).astype(BF16)
        packed = jnp.zeros((REQ, 128), F32)
        for j in range(4):
            for at, part in enumerate(stats):
                packed = jnp.where(lane16 == 6 * j + at, part[4 * p + j], packed)
        part_send[p, :, 256:384] = packed.astype(BF16)
    for d in (4, 3, 5, 2, 6, 1, 7):
        to = (t + d) % 8
        send(part_send.at[to], part_recv.at[t], z_send.at[1], z_recv.at[1], z_peer[d])

    arrived(nodes.at[pl.ds(0, 30)], d_send)
    arrived(nodes.at[pl.ds(0, 32)], s_send)
    arrived(q_all.at[pl.ds(0, 7)], z_send.at[0])
    @pl.when(t // 2 != t)
    def _():
        arrived(kv_recv.at[0], kv_rs.at[0])

    @pl.when(KV_HEADS + t // 2 != t)
    def _():
        arrived(kv_recv.at[1], kv_rs.at[1])

    queries = q_all[t].astype(F32)
    token_key = kv_recv[0].astype(F32)
    token_value = kv_recv[1].astype(F32)
    token_score = jnp.zeros((REQ, 128), F32)
    for j in range(4):
        product = queries[:, j // 2 * 128 : j // 2 * 128 + 128] * token_key
        product = jnp.where(low_half if j % 2 == 0 else jnp.logical_not(low_half), product, 0.0)
        token_score = jnp.where(lane16 == 6 * j, jnp.sum(product, axis=-1, keepdims=True), token_score)

    part_recv[t] = part_send[t]
    arrived(part_recv.at[pl.ds(0, 7)], z_recv.at[1])

    maxima, totals = [], []
    for s in range(8):
        stat = part_recv[s, :, 256:384].astype(F32)
        stat = stat + pltpu.roll(stat, 127, 1) + pltpu.roll(stat, 126, 1)
        maxima.append(stat)
        totals.append(pltpu.roll(stat, 125, 1))
    upper = token_score
    for entry in maxima:
        upper = jnp.maximum(upper, entry)
    fresh = jnp.exp(token_score - upper)
    total = fresh
    factors = []
    for entry, share in zip(maxima, totals):
        factors.append(jnp.exp(entry - upper))
        total = total + share * factors[-1]

    def widen(value, b):
        return jnp.where(low_half, value[:, 12 * b : 12 * b + 1], value[:, 12 * b + 6 : 12 * b + 7])

    halves = []
    for b in range(2):
        summed = widen(fresh.astype(BF16).astype(F32), b) * token_value
        for s in range(8):
            summed = summed + part_recv[s, :, 128 * b : 128 * b + 128].astype(F32) * widen(factors[s], b)
        halves.append((summed / widen(total, b)).astype(BF16))
    attention = jnp.concatenate(halves, axis=1)

    locals_[5].wait()
    for d in (4, 3, 5, 2, 6, 1, 7, 0):
        to = (t + d) % 8
        block = dot(attention, v_wo[:, pl.ds(pl.multiple_of(to * 256, 256), 256)]).astype(BF16)
        if d:
            rs_send[to] = block
            send(rs_send.at[to], rs_recv.at[t], z_send.at[2], z_recv.at[2], z_peer[d])
        else:
            rs_recv[t] = block
    arrived(rs_recv.at[pl.ds(0, 7)], z_recv.at[2])
    result = v_hid[:, pl.ds(pl.multiple_of(t * 256, 256), 256)].astype(F32)
    for s in range(8):
        result = result + rs_recv[s].astype(F32)
    out_h[...] = result.astype(BF16)

    arrived(part_send.at[pl.ds(0, 7)], z_send.at[1])
    arrived(rs_send.at[pl.ds(0, 7)], z_send.at[2])
    for j in range(2):
        target = (t % KV_HEADS) * 2 + j

        @pl.when(target != t)
        def _():
            pltpu.make_async_copy(kv_send, kv_send, kv_ss.at[j]).wait()


def on_device(
    hidden_in, norm_gain, w_query, w_keyval, w_output, prefix_cache, private_cache,
    node_parent, node_length, request_node, private_length,
):
    anywhere = pl.BlockSpec(memory_space=pltpu.HBM)
    scalars = pl.BlockSpec(memory_space=pltpu.SMEM)
    vector = pl.BlockSpec(memory_space=pltpu.VMEM)
    dma = pltpu.SemaphoreType.DMA
    return pl.pallas_call(
        kernel,
        out_shape=(
            jax.ShapeDtypeStruct((REQ, 256), BF16),
            jax.ShapeDtypeStruct((REQ, HEAD_DIM), BF16),
        ),
        in_specs=[anywhere] * 7 + [scalars] * 4,
        out_specs=(vector, vector),
        scratch_shapes=[
            pltpu.VMEM((REQ, 2048), BF16),
            pltpu.VMEM((2048,), BF16),
            pltpu.VMEM((2048, 256), BF16),
            pltpu.VMEM((64, 2048), BF16),
            pltpu.VMEM((256, 2048), BF16),
            pltpu.VMEM((REQ, SLOTS, 512), BF16),
            pltpu.VMEM((64, SLOTS, 512), BF16),
            pltpu.VMEM((8, REQ, 256), BF16),
            pltpu.VMEM((REQ, 128), BF16),
            pltpu.VMEM((2, REQ, 128), BF16),
            pltpu.VMEM((8, REQ, 384), BF16),
            pltpu.VMEM((8, REQ, 384), BF16),
            pltpu.VMEM((8, REQ, 256), BF16),
            pltpu.VMEM((8, REQ, 256), BF16),
            dma((7,)),
            dma,
            dma((2, 4, 4)),
            dma,
            dma,
            dma((3,)),
            dma((3,)),
            dma((2,)),
            dma((2,)),
        ],
        compiler_params=pltpu.CompilerParams(
            collective_id=0, has_side_effects=True, vmem_limit_bytes=40 * 1024 * 1024
        ),
    )(
        *(
            pltpu.with_memory_space_constraint(array, pltpu.HBM)
            for array in (
                hidden_in, norm_gain, w_query, w_keyval.T, w_output, prefix_cache, private_cache,
                node_parent, node_length, request_node, private_length,
            )
        )
    )


def solution(mesh):
    placed = (
        P("grp", None), P(), P(None, "tp"), P(None, "tp"), P("tp", None), P("grp", "tp", None),
        P("grp", "tp", None), P(), P(), P(), P("grp"),
    )
    return jax.shard_map(
        on_device, mesh=mesh, in_specs=placed, out_specs=(P("grp", "tp"), P("grp", "tp")), check_vma=False
    )
```

```python
import math

import jax
import jax.numpy as jnp
from jax import lax
from jax.experimental import pallas as pl
from jax.experimental.pallas import tpu as pltpu
from jax.sharding import PartitionSpec as P

MESH = pl.DeviceIdType.MESH
F32 = jnp.float32
BF16 = jnp.bfloat16
HEADS = 32
KV_HEADS = 4
HEAD_DIM = 64
REQ = 16
SLOTS = 64
ROWS = HEADS * REQ
KW = KV_HEADS * HEAD_DIM
LOW = -1e30


def dot(a, b):
    return jnp.dot(a, b, preferred_element_type=F32)


def dot_t(a, b):
    return lax.dot_general(a, b, (((1,), (1,)), ((), ())), preferred_element_type=F32)


def three_parts(value):
    first = value.astype(BF16).astype(F32)
    rest = value - first
    second = rest.astype(BF16).astype(F32)
    third = (rest - second).astype(BF16).astype(F32)
    return first, second, third


def rope_tables(position):
    lane = lax.broadcasted_iota(jnp.int32, (REQ, 128), 1)
    index = (lane % (HEAD_DIM // 2)).astype(F32)
    frequency = jnp.exp(index * (-2.0 * math.log(10000.0) / HEAD_DIM))
    angle = position * frequency
    front = lane % HEAD_DIM < HEAD_DIM // 2
    sine = jnp.sin(angle)
    return jnp.cos(angle), jnp.where(front, -sine, sine), front


def rope(block, tables):
    cosine, sine, front = tables
    half = HEAD_DIM // 2
    swapped = jnp.where(front, pltpu.roll(block, 128 - half, 1), pltpu.roll(block, half, 1))
    return block * cosine + swapped * sine


def kernel(
    hid, gain, wq, wkv, wo, prefix, private, parent, nlen, reqnode, plen,
    out_h, out_kv,
    v_hid, v_gain, v_wq, v_wkv, v_wo, v_priv, nodes,
    q_all, kv_send, kv_recv, part_send, part_recv, rs_send, rs_recv,
    l_sem, d_send, d_recv, s_send, s_recv, z_send, z_recv, kv_ss, kv_rs,
):
    g = lax.axis_index("grp")
    t = lax.axis_index("tp")
    x, y, c = g // 8, (g // 2) % 4, g % 2

    def group(xx, yy, cc):
        return (xx * 4 + yy) * 2 + cc

    def chunk(xx, yy, cc):
        return nodes.at[pl.ds(group(xx, yy, cc) * 2, 2)]

    x_peer = {d: (group((x + 4 + d * (1 - 2 * c)) % 4, y, c), t) for d in (1, 2, -1)}
    y_peer = {d: (group(x, (y + 4 + d * (1 - 2 * c)) % 4, c), t) for d in (1, 2, -1)}
    sibling = (group(x, y, 1 - c), t)
    z_peer = [(g, (t + d) % 8) for d in range(8)]
    everyone = list(x_peer.values()) + list(y_peer.values()) + [sibling] + z_peer[1:]

    barrier = pltpu.get_barrier_semaphore()
    for peer in everyone:
        pl.semaphore_signal(barrier, inc=1, device_id=peer, device_id_type=MESH)

    locals_ = []
    for k, (src, dst) in enumerate(
        ((hid, v_hid), (gain, v_gain), (wq, v_wq), (wkv, v_wkv), (private, v_priv), (wo, v_wo),
         (prefix, chunk(x, y, c)))
    ):
        copy = pltpu.make_async_copy(src, dst, l_sem.at[k])
        copy.start()
        locals_.append(copy)

    def send(src, dst, ssem, rsem, peer):
        pltpu.make_async_remote_copy(
            src_ref=src, dst_ref=dst, send_sem=ssem, recv_sem=rsem, device_id=peer, device_id_type=MESH
        ).start()

    def arrived(ref, sem):
        pltpu.make_async_copy(ref, ref, sem).wait()

    turn = 1 - 2 * c

    def slab(i, a, b):
        return nodes.at[pl.ds(group((x + 16 - turn * a) % 4, (y + 16 - turn * b) % 4, c) * 2 + i, 1)]

    def hand_on(i, a, b, *ways):
        block = prefix.at[pl.ds(i, 1)] if a + b == 0 else slab(i, a, b)
        for axis, step in ways:
            if axis == "s":
                send(block, slab(i, a, b), s_send, s_recv, sibling)
                continue
            aa, bb = ((a + step) % 4, b) if axis == "x" else (a, (b + step) % 4)
            peer = (x_peer if axis == "x" else y_peer)[step]
            send(block, slab(i, a, b), d_send, d_recv.at[i, aa, bb], peer)

    def relay(i, a, b, *ways):
        if i == 1:
            a, b = b, a
            ways = [({"x": "y", "y": "x"}[axis], step) for axis, step in ways]
        if a + b:
            arrived(slab(i, a, b), d_recv.at[i, a, b])
        hand_on(i, a, b, *ways, ("s", 0))

    pl.semaphore_wait(barrier, len(everyone))
    hand_on(0, 0, 0, ("x", 1), ("x", -1))
    hand_on(1, 0, 0, ("y", 1), ("y", -1))
    hand_on(0, 0, 0, ("x", 2))
    hand_on(1, 0, 0, ("y", 2))
    hand_on(0, 0, 0, ("y", 1), ("y", -1), ("s", 0))
    hand_on(1, 0, 0, ("x", 1), ("x", -1), ("s", 0))

    mids = [reqnode[g * REQ + r] for r in range(REQ)]
    root = parent[mids[0]]
    root_length = nlen[root]
    row16 = lax.broadcasted_iota(jnp.int32, (REQ, 128), 0)
    lane16 = lax.broadcasted_iota(jnp.int32, (REQ, 128), 1)
    private_length = jnp.zeros((REQ, 128), jnp.int32)
    mid_length = jnp.zeros((REQ, 128), jnp.int32)
    for r in range(REQ):
        private_length = jnp.where(row16 == r, plen[r], private_length)
        mid_length = jnp.where(row16 == r, nlen[mids[r]], mid_length)
    tables = rope_tables((private_length + mid_length + root_length).astype(F32))

    locals_[0].wait()
    locals_[1].wait()
    floats = v_hid[...].astype(F32)
    spread = jnp.mean(floats * floats, axis=-1, keepdims=True)
    normed = (floats * lax.rsqrt(spread + 1e-05) * v_gain[...].reshape(1, 2048).astype(F32)).astype(BF16)
    locals_[2].wait()
    query = dot(normed, v_wq[...])
    for half in range(2):
        piece = rope(query[:, half * 128 : half * 128 + 128], tables).astype(BF16)
        q_all[t, :, half * 128 : half * 128 + 128] = piece * jnp.asarray(HEAD_DIM**-0.5, BF16)
    locals_[3].wait()
    keyval = dot_t(normed, v_wkv[...])
    doubled = jnp.concatenate([keyval, keyval], axis=1)
    keyval = jnp.where(t < KV_HEADS, rope(doubled, tables), doubled).astype(BF16)
    out_kv[...] = keyval[:, :HEAD_DIM]
    kv_send[...] = keyval
    for d in (4, 3, 5, 2, 6, 1, 7):
        send(q_all.at[t], q_all.at[t], z_send.at[0], z_recv.at[0], z_peer[d])
    kind = t // KV_HEADS
    for j in range(2):
        target = (t % KV_HEADS) * 2 + j

        @pl.when(target != t)
        def _():
            pltpu.make_async_remote_copy(
                src_ref=kv_send, dst_ref=kv_recv.at[kind], send_sem=kv_ss.at[j],
                recv_sem=kv_rs.at[kind], device_id=(g, target), device_id_type=MESH,
            ).start()

        @pl.when(target == t)
        def _():
            kv_recv[kind] = kv_send[...]

    def relay_first():
        for a in (1, 3):
            for i in range(2):
                relay(i, a, 0, ("y", 1), ("y", -1))
        for i in range(2):
            relay(i, 2, 0, ("y", 2), ("y", 1), ("y", -1))

    def relay_second():
        for i in range(2):
            relay(i, 0, 1, ("y", 1))
            relay(i, 0, 3)
        for i in range(2):
            relay(i, 1, 1, ("y", 1))
            relay(i, 3, 3, ("y", -1))

    def relay_last():
        for where in ((1, 3), (3, 1), (2, 1), (2, 3), (0, 2), (2, 2), (1, 2), (3, 2)):
            for i in range(2):
                relay(i, *where)
        arrived(nodes.at[pl.ds(0, 32)], s_recv)

    relay_first()

    arrived(q_all.at[pl.ds(0, 7)], z_recv.at[0])
    lane256 = lax.broadcasted_iota(jnp.int32, (REQ, KW), 1)
    pieces = []
    for h in range(HEADS):
        j, k = h % 4, h // 8
        four = q_all[h // 4].astype(F32)
        shift = ((k - j) * HEAD_DIM) % KW
        if shift:
            four = pltpu.roll(four, shift, 1)
        pieces.append(jnp.where(lane256 // HEAD_DIM == k, four, 0.0).astype(BF16))
    blocked = jnp.concatenate(pieces, axis=0)

    relay_second()
    lane3 = lax.broadcasted_iota(jnp.int32, (1, REQ, 128), 2)
    row3 = lax.broadcasted_iota(jnp.int32, (1, REQ, 128), 1)
    slot3 = lane3 % SLOTS + t * SLOTS
    own_half = lane3 // SLOTS == row3 % 2
    shape3 = (HEADS, REQ, 128)

    def pair_mask(pair, half):
        return (row3 // 2 == pair) & half

    def compact(key_quad, half, so_far):
        for q in range(4):
            wide = dot_t(blocked, key_quad(q))
            for e in range(2):
                block = wide[:, e * 128 : e * 128 + 128].reshape(shape3)
                so_far = jnp.where(pair_mask(q * 2 + e, half), block, so_far)
        return so_far

    def weigh(weights, value_quad, half):
        total = None
        for q in range(4):
            wide = jnp.concatenate(
                [
                    jnp.where(pair_mask(q * 2 + e, half), weights, 0.0).astype(BF16).reshape(ROWS, 128)
                    for e in range(2)
                ],
                axis=1,
            )
            term = dot(wide, value_quad(q))
            total = term if total is None else total + term
        return total

    def softmax_part(scores, valid):
        scores = jnp.where(valid, scores, LOW)
        maxima = jnp.max(scores, axis=-1, keepdims=True)
        weights = jnp.where(valid, jnp.exp(scores - maxima), 0.0)
        return weights, maxima, jnp.sum(weights, axis=-1, keepdims=True)

    locals_[4].wait()

    def own_rows(q, lanes):
        return v_priv[q * 4 : q * 4 + 4, :, lanes].reshape(4 * SLOTS, KW)

    keys, values = pl.ds(0, KW), pl.ds(KW, KW)
    scores = compact(lambda q: own_rows(q, keys), own_half, jnp.zeros(shape3, F32))
    valid = own_half & (slot3 < private_length.reshape(1, REQ, 128))
    weights, own_max, own_total = softmax_part(scores, valid)
    own_sum = weigh(weights, lambda q: own_rows(q, values), own_half)

    relay_last()
    locals_[6].wait()

    def node_rows(q, lanes):
        order = (q * 4 + 1, q * 4, q * 4 + 3, q * 4 + 2)
        return jnp.concatenate([nodes[mids[r], :, lanes] for r in order], axis=0)

    root_keys = nodes[root, :, keys]
    root_values = nodes[root, :, values]
    root_scores = dot_t(blocked, jnp.concatenate([root_keys, root_keys], axis=0)).reshape(shape3)
    node_half = jnp.logical_not(own_half)
    scores = compact(lambda q: node_rows(q, keys), node_half, root_scores)
    limit = jnp.where(node_half, mid_length.reshape(1, REQ, 128), root_length)
    weights, tree_max, tree_total = softmax_part(scores, slot3 < limit)
    tree_sum = weigh(weights, lambda q: node_rows(q, values), node_half)
    tree_sum = tree_sum + dot(
        jnp.where(own_half, weights, 0.0).astype(BF16).reshape(ROWS, 128),
        jnp.concatenate([root_values, root_values], axis=0),
    )

    upper = jnp.maximum(own_max, tree_max)
    own_scale, tree_scale = jnp.exp(own_max - upper), jnp.exp(tree_max - upper)
    total = own_total * own_scale + tree_total * tree_scale
    stats = three_parts(upper) + three_parts(total)
    low_half = lane16 < HEAD_DIM
    for p in range(8):
        for b in range(2):
            pair = []
            for e in range(2):
                h = 4 * p + 2 * b + e
                k = h // 8
                rows, lanes = slice(REQ * h, REQ * h + REQ), slice(128 * (k // 2), 128 * (k // 2) + 128)
                piece = own_sum[rows, lanes] * own_scale[h] + tree_sum[rows, lanes] * tree_scale[h]
                pair.append(piece if k % 2 == e else pltpu.roll(piece, HEAD_DIM, 1))
            part_send[p, :, 128 * b : 128 * b + 128] = jnp.where(low_half, *pair).astype(BF16)
        packed = jnp.zeros((REQ, 128), F32)
        for j in range(4):
            for at, part in enumerate(stats):
                packed = jnp.where(lane16 == 6 * j + at, part[4 * p + j], packed)
        part_send[p, :, 256:384] = packed.astype(BF16)
    for d in (4, 3, 5, 2, 6, 1, 7):
        to = (t + d) % 8
        send(part_send.at[to], part_recv.at[t], z_send.at[1], z_recv.at[1], z_peer[d])

    arrived(nodes.at[pl.ds(0, 30)], d_send)
    arrived(nodes.at[pl.ds(0, 32)], s_send)
    arrived(q_all.at[pl.ds(0, 7)], z_send.at[0])
    @pl.when(t // 2 != t)
    def _():
        arrived(kv_recv.at[0], kv_rs.at[0])

    @pl.when(KV_HEADS + t // 2 != t)
    def _():
        arrived(kv_recv.at[1], kv_rs.at[1])

    queries = q_all[t].astype(F32)
    token_key = kv_recv[0].astype(F32)
    token_value = kv_recv[1].astype(F32)
    token_score = jnp.zeros((REQ, 128), F32)
    for j in range(4):
        product = queries[:, j // 2 * 128 : j // 2 * 128 + 128] * token_key
        product = jnp.where(low_half if j % 2 == 0 else jnp.logical_not(low_half), product, 0.0)
        token_score = jnp.where(lane16 == 6 * j, jnp.sum(product, axis=-1, keepdims=True), token_score)

    part_recv[t] = part_send[t]
    arrived(part_recv.at[pl.ds(0, 7)], z_recv.at[1])

    maxima, totals = [], []
    for s in range(8):
        stat = part_recv[s, :, 256:384].astype(F32)
        stat = stat + pltpu.roll(stat, 127, 1) + pltpu.roll(stat, 126, 1)
        maxima.append(stat)
        totals.append(pltpu.roll(stat, 125, 1))
    upper = token_score
    for entry in maxima:
        upper = jnp.maximum(upper, entry)
    fresh = jnp.exp(token_score - upper)
    total = fresh
    factors = []
    for entry, share in zip(maxima, totals):
        factors.append(jnp.exp(entry - upper))
        total = total + share * factors[-1]

    def widen(value, b):
        return jnp.where(low_half, value[:, 12 * b : 12 * b + 1], value[:, 12 * b + 6 : 12 * b + 7])

    halves = []
    for b in range(2):
        summed = widen(fresh.astype(BF16).astype(F32), b) * token_value
        for s in range(8):
            summed = summed + part_recv[s, :, 128 * b : 128 * b + 128].astype(F32) * widen(factors[s], b)
        halves.append((summed / widen(total, b)).astype(BF16))
    attention = jnp.concatenate(halves, axis=1)

    locals_[5].wait()
    for d in (4, 3, 5, 2, 6, 1, 7, 0):
        to = (t + d) % 8
        block = dot(attention, v_wo[:, pl.ds(pl.multiple_of(to * 256, 256), 256)]).astype(BF16)
        if d:
            rs_send[to] = block
            send(rs_send.at[to], rs_recv.at[t], z_send.at[2], z_recv.at[2], z_peer[d])
        else:
            rs_recv[t] = block
    arrived(rs_recv.at[pl.ds(0, 7)], z_recv.at[2])
    result = v_hid[:, pl.ds(pl.multiple_of(t * 256, 256), 256)].astype(F32)
    for s in range(8):
        result = result + rs_recv[s].astype(F32)
    out_h[...] = result.astype(BF16)

    arrived(part_send.at[pl.ds(0, 7)], z_send.at[1])
    arrived(rs_send.at[pl.ds(0, 7)], z_send.at[2])
    for j in range(2):
        target = (t % KV_HEADS) * 2 + j

        @pl.when(target != t)
        def _():
            pltpu.make_async_copy(kv_send, kv_send, kv_ss.at[j]).wait()


def on_device(
    hidden_in, norm_gain, w_query, w_keyval, w_output, prefix_cache, private_cache,
    node_parent, node_length, request_node, private_length,
):
    anywhere = pl.BlockSpec(memory_space=pltpu.HBM)
    scalars = pl.BlockSpec(memory_space=pltpu.SMEM)
    vector = pl.BlockSpec(memory_space=pltpu.VMEM)
    dma = pltpu.SemaphoreType.DMA
    return pl.pallas_call(
        kernel,
        out_shape=(
            jax.ShapeDtypeStruct((REQ, 256), BF16),
            jax.ShapeDtypeStruct((REQ, HEAD_DIM), BF16),
        ),
        in_specs=[anywhere] * 7 + [scalars] * 4,
        out_specs=(vector, vector),
        scratch_shapes=[
            pltpu.VMEM((REQ, 2048), BF16),
            pltpu.VMEM((2048,), BF16),
            pltpu.VMEM((2048, 256), BF16),
            pltpu.VMEM((64, 2048), BF16),
            pltpu.VMEM((256, 2048), BF16),
            pltpu.VMEM((REQ, SLOTS, 512), BF16),
            pltpu.VMEM((64, SLOTS, 512), BF16),
            pltpu.VMEM((8, REQ, 256), BF16),
            pltpu.VMEM((REQ, 128), BF16),
            pltpu.VMEM((2, REQ, 128), BF16),
            pltpu.VMEM((8, REQ, 384), BF16),
            pltpu.VMEM((8, REQ, 384), BF16),
            pltpu.VMEM((8, REQ, 256), BF16),
            pltpu.VMEM((8, REQ, 256), BF16),
            dma((7,)),
            dma,
            dma((2, 4, 4)),
            dma,
            dma,
            dma((3,)),
            dma((3,)),
            dma((2,)),
            dma((2,)),
        ],
        compiler_params=pltpu.CompilerParams(
            collective_id=0, has_side_effects=True, vmem_limit_bytes=40 * 1024 * 1024
        ),
    )(
        *(
            pltpu.with_memory_space_constraint(array, pltpu.HBM)
            for array in (
                hidden_in, norm_gain, w_query, w_keyval.T, w_output, prefix_cache, private_cache,
                node_parent, node_length, request_node, private_length,
            )
        )
    )


def solution(mesh):
    placed = (
        P("grp", None), P(), P(None, "tp"), P(None, "tp"), P("tp", None), P("grp", "tp", None),
        P("grp", "tp", None), P(), P(), P(), P("grp"),
    )
    return jax.shard_map(
        on_device, mesh=mesh, in_specs=placed, out_specs=(P("grp", "tp"), P("grp", "tp")), check_vma=False
    )
```

```python
import math

import jax
import jax.numpy as jnp
from jax import lax
from jax.experimental import pallas as pl
from jax.experimental.pallas import tpu as pltpu
from jax.sharding import PartitionSpec as P

MESH = pl.DeviceIdType.MESH
F32 = jnp.float32
BF16 = jnp.bfloat16
HEADS = 32
KV_HEADS = 4
HEAD_DIM = 64
REQ = 16
SLOTS = 64
ROWS = HEADS * REQ
KW = KV_HEADS * HEAD_DIM
LOW = -1e30


def dot(a, b):
    return jnp.dot(a, b, preferred_element_type=F32)


def dot_t(a, b):
    return lax.dot_general(a, b, (((1,), (1,)), ((), ())), preferred_element_type=F32)


def three_parts(value):
    first = value.astype(BF16).astype(F32)
    rest = value - first
    second = rest.astype(BF16).astype(F32)
    third = (rest - second).astype(BF16).astype(F32)
    return first, second, third


def rope_tables(position):
    lane = lax.broadcasted_iota(jnp.int32, (REQ, 128), 1)
    index = (lane % (HEAD_DIM // 2)).astype(F32)
    frequency = jnp.exp(index * (-2.0 * math.log(10000.0) / HEAD_DIM))
    angle = position * frequency
    front = lane % HEAD_DIM < HEAD_DIM // 2
    sine = jnp.sin(angle)
    return jnp.cos(angle), jnp.where(front, -sine, sine), front


def rope(block, tables):
    cosine, sine, front = tables
    half = HEAD_DIM // 2
    swapped = jnp.where(front, pltpu.roll(block, 128 - half, 1), pltpu.roll(block, half, 1))
    return block * cosine + swapped * sine


def kernel(
    hid, gain, wq, wkv, wo, prefix, private, parent_in, nlen_in, reqnode_in, plen_in,
    out_h, out_kv,
    v_hid, v_gain, v_wq, v_wkv, v_wo, v_priv, parent, nlen, reqnode, plen, nodes,
    q_all, kv_send, kv_recv, part_send, part_recv, rs_send, rs_recv,
    l_sem, d_send, d_recv, s_send, s_recv, z_send, z_recv, kv_ss, kv_rs,
):
    g = lax.axis_index("grp")
    t = lax.axis_index("tp")
    x, y, c = g // 8, (g // 2) % 4, g % 2

    def group(xx, yy, cc):
        return (xx * 4 + yy) * 2 + cc

    def chunk(xx, yy, cc):
        return nodes.at[pl.ds(group(xx, yy, cc) * 2, 2)]

    x_peer = {d: (group((x + 4 + d * (1 - 2 * c)) % 4, y, c), t) for d in (1, 2, -1)}
    y_peer = {d: (group(x, (y + 4 + d * (1 - 2 * c)) % 4, c), t) for d in (1, 2, -1)}
    sibling = (group(x, y, 1 - c), t)
    z_peer = [(g, (t + d) % 8) for d in range(8)]
    everyone = list(x_peer.values()) + list(y_peer.values()) + [sibling] + z_peer[1:]

    barrier = pltpu.get_barrier_semaphore()
    for peer in everyone:
        pl.semaphore_signal(barrier, inc=1, device_id=peer, device_id_type=MESH)

    locals_ = []
    for k, (src, dst) in enumerate(
        ((hid, v_hid), (gain, v_gain), (wq, v_wq), (wkv, v_wkv), (private, v_priv), (wo, v_wo),
         (prefix, chunk(x, y, c)), (parent_in, parent), (nlen_in, nlen), (reqnode_in, reqnode), (plen_in, plen))
    ):
        copy = pltpu.make_async_copy(src, dst, l_sem.at[k])
        copy.start()
        locals_.append(copy)

    def send(src, dst, ssem, rsem, peer):
        pltpu.make_async_remote_copy(
            src_ref=src, dst_ref=dst, send_sem=ssem, recv_sem=rsem, device_id=peer, device_id_type=MESH
        ).start()

    def arrived(ref, sem):
        pltpu.make_async_copy(ref, ref, sem).wait()

    turn = 1 - 2 * c

    def slab(i, a, b):
        return nodes.at[pl.ds(group((x + 16 - turn * a) % 4, (y + 16 - turn * b) % 4, c) * 2 + i, 1)]

    def hand_on(i, a, b, *ways):
        block = prefix.at[pl.ds(i, 1)] if a + b == 0 else slab(i, a, b)
        for axis, step in ways:
            if axis == "s":
                send(block, slab(i, a, b), s_send, s_recv, sibling)
                continue
            aa, bb = ((a + step) % 4, b) if axis == "x" else (a, (b + step) % 4)
            peer = (x_peer if axis == "x" else y_peer)[step]
            send(block, slab(i, a, b), d_send, d_recv.at[i, aa, bb], peer)

    def relay(i, a, b, *ways):
        if i == 1:
            a, b = b, a
            ways = [({"x": "y", "y": "x"}[axis], step) for axis, step in ways]
        if a + b:
            arrived(slab(i, a, b), d_recv.at[i, a, b])
        hand_on(i, a, b, *ways, ("s", 0))

    pl.semaphore_wait(barrier, len(everyone))
    hand_on(0, 0, 0, ("x", 1), ("x", -1))
    hand_on(1, 0, 0, ("y", 1), ("y", -1))
    hand_on(0, 0, 0, ("x", 2))
    hand_on(1, 0, 0, ("y", 2))
    hand_on(0, 0, 0, ("y", 1), ("y", -1), ("s", 0))
    hand_on(1, 0, 0, ("x", 1), ("x", -1), ("s", 0))

    for k in range(7, 11):
        locals_[k].wait()
    mids = [reqnode[g * REQ + r] for r in range(REQ)]
    root = parent[mids[0]]
    root_length = nlen[root]
    row16 = lax.broadcasted_iota(jnp.int32, (REQ, 128), 0)
    lane16 = lax.broadcasted_iota(jnp.int32, (REQ, 128), 1)
    private_length = jnp.zeros((REQ, 128), jnp.int32)
    mid_length = jnp.zeros((REQ, 128), jnp.int32)
    for r in range(REQ):
        private_length = jnp.where(row16 == r, plen[r], private_length)
        mid_length = jnp.where(row16 == r, nlen[mids[r]], mid_length)
    tables = rope_tables((private_length + mid_length + root_length).astype(F32))

    locals_[0].wait()
    locals_[1].wait()
    floats = v_hid[...].astype(F32)
    spread = jnp.mean(floats * floats, axis=-1, keepdims=True)
    normed = (floats * lax.rsqrt(spread + 1e-05) * v_gain[...].reshape(1, 2048).astype(F32)).astype(BF16)
    locals_[2].wait()
    query = dot(normed, v_wq[...])
    for half in range(2):
        piece = rope(query[:, half * 128 : half * 128 + 128], tables).astype(BF16)
        q_all[t, :, half * 128 : half * 128 + 128] = piece * jnp.asarray(HEAD_DIM**-0.5, BF16)
    locals_[3].wait()
    keyval = dot_t(normed, v_wkv[...])
    doubled = jnp.concatenate([keyval, keyval], axis=1)
    keyval = jnp.where(t < KV_HEADS, rope(doubled, tables), doubled).astype(BF16)
    out_kv[...] = keyval[:, :HEAD_DIM]
    kv_send[...] = keyval
    for d in (4, 3, 5, 2, 6, 1, 7):
        send(q_all.at[t], q_all.at[t], z_send.at[0], z_recv.at[0], z_peer[d])
    kind = t // KV_HEADS
    for j in range(2):
        target = (t % KV_HEADS) * 2 + j

        @pl.when(target != t)
        def _():
            pltpu.make_async_remote_copy(
                src_ref=kv_send, dst_ref=kv_recv.at[kind], send_sem=kv_ss.at[j],
                recv_sem=kv_rs.at[kind], device_id=(g, target), device_id_type=MESH,
            ).start()

        @pl.when(target == t)
        def _():
            kv_recv[kind] = kv_send[...]

    def relay_first():
        for a in (1, 3):
            for i in range(2):
                relay(i, a, 0, ("y", 1), ("y", -1))
        for i in range(2):
            relay(i, 2, 0, ("y", 2), ("y", 1), ("y", -1))

    def relay_second():
        for i in range(2):
            relay(i, 0, 1, ("y", 1))
            relay(i, 0, 3)
        for i in range(2):
            relay(i, 1, 1, ("y", 1))
            relay(i, 3, 3, ("y", -1))

    def relay_last():
        for where in ((1, 3), (3, 1), (2, 1), (2, 3), (0, 2), (2, 2), (1, 2), (3, 2)):
            for i in range(2):
                relay(i, *where)
        arrived(nodes.at[pl.ds(0, 32)], s_recv)

    relay_first()

    arrived(q_all.at[pl.ds(0, 7)], z_recv.at[0])
    lane256 = lax.broadcasted_iota(jnp.int32, (REQ, KW), 1)
    pieces = []
    for h in range(HEADS):
        j, k = h % 4, h // 8
        four = q_all[h // 4].astype(F32)
        shift = ((k - j) * HEAD_DIM) % KW
        if shift:
            four = pltpu.roll(four, shift, 1)
        pieces.append(jnp.where(lane256 // HEAD_DIM == k, four, 0.0).astype(BF16))
    blocked = jnp.concatenate(pieces, axis=0)

    relay_second()
    lane3 = lax.broadcasted_iota(jnp.int32, (1, REQ, 128), 2)
    row3 = lax.broadcasted_iota(jnp.int32, (1, REQ, 128), 1)
    slot3 = lane3 % SLOTS + t * SLOTS
    own_half = lane3 // SLOTS == row3 % 2
    shape3 = (HEADS, REQ, 128)

    def pair_mask(pair, half):
        return (row3 // 2 == pair) & half

    def compact(key_quad, half, so_far):
        for q in range(4):
            wide = dot_t(blocked, key_quad(q))
            for e in range(2):
                block = wide[:, e * 128 : e * 128 + 128].reshape(shape3)
                so_far = jnp.where(pair_mask(q * 2 + e, half), block, so_far)
        return so_far

    def weigh(weights, value_quad, half):
        total = None
        for q in range(4):
            wide = jnp.concatenate(
                [
                    jnp.where(pair_mask(q * 2 + e, half), weights, 0.0).astype(BF16).reshape(ROWS, 128)
                    for e in range(2)
                ],
                axis=1,
            )
            term = dot(wide, value_quad(q))
            total = term if total is None else total + term
        return total

    def softmax_part(scores, valid):
        scores = jnp.where(valid, scores, LOW)
        maxima = jnp.max(scores, axis=-1, keepdims=True)
        weights = jnp.where(valid, jnp.exp(scores - maxima), 0.0)
        return weights, maxima, jnp.sum(weights, axis=-1, keepdims=True)

    locals_[4].wait()

    def own_rows(q, lanes):
        return v_priv[q * 4 : q * 4 + 4, :, lanes].reshape(4 * SLOTS, KW)

    keys, values = pl.ds(0, KW), pl.ds(KW, KW)
    scores = compact(lambda q: own_rows(q, keys), own_half, jnp.zeros(shape3, F32))
    valid = own_half & (slot3 < private_length.reshape(1, REQ, 128))
    weights, own_max, own_total = softmax_part(scores, valid)
    own_sum = weigh(weights, lambda q: own_rows(q, values), own_half)

    relay_last()
    locals_[6].wait()

    def node_rows(q, lanes):
        order = (q * 4 + 1, q * 4, q * 4 + 3, q * 4 + 2)
        return jnp.concatenate([nodes[mids[r], :, lanes] for r in order], axis=0)

    root_keys = nodes[root, :, keys]
    root_values = nodes[root, :, values]
    root_scores = dot_t(blocked, jnp.concatenate([root_keys, root_keys], axis=0)).reshape(shape3)
    node_half = jnp.logical_not(own_half)
    scores = compact(lambda q: node_rows(q, keys), node_half, root_scores)
    limit = jnp.where(node_half, mid_length.reshape(1, REQ, 128), root_length)
    weights, tree_max, tree_total = softmax_part(scores, slot3 < limit)
    tree_sum = weigh(weights, lambda q: node_rows(q, values), node_half)
    tree_sum = tree_sum + dot(
        jnp.where(own_half, weights, 0.0).astype(BF16).reshape(ROWS, 128),
        jnp.concatenate([root_values, root_values], axis=0),
    )

    upper = jnp.maximum(own_max, tree_max)
    own_scale, tree_scale = jnp.exp(own_max - upper), jnp.exp(tree_max - upper)
    total = own_total * own_scale + tree_total * tree_scale
    stats = three_parts(upper) + three_parts(total)
    low_half = lane16 < HEAD_DIM
    for p in range(8):
        for b in range(2):
            pair = []
            for e in range(2):
                h = 4 * p + 2 * b + e
                k = h // 8
                rows, lanes = slice(REQ * h, REQ * h + REQ), slice(128 * (k // 2), 128 * (k // 2) + 128)
                piece = own_sum[rows, lanes] * own_scale[h] + tree_sum[rows, lanes] * tree_scale[h]
                pair.append(piece if k % 2 == e else pltpu.roll(piece, HEAD_DIM, 1))
            part_send[p, :, 128 * b : 128 * b + 128] = jnp.where(low_half, *pair).astype(BF16)
        packed = jnp.zeros((REQ, 128), F32)
        for j in range(4):
            for at, part in enumerate(stats):
                packed = jnp.where(lane16 == 6 * j + at, part[4 * p + j], packed)
        part_send[p, :, 256:384] = packed.astype(BF16)
    for d in (4, 3, 5, 2, 6, 1, 7):
        to = (t + d) % 8
        send(part_send.at[to], part_recv.at[t], z_send.at[1], z_recv.at[1], z_peer[d])

    arrived(nodes.at[pl.ds(0, 30)], d_send)
    arrived(nodes.at[pl.ds(0, 32)], s_send)
    arrived(q_all.at[pl.ds(0, 7)], z_send.at[0])
    @pl.when(t // 2 != t)
    def _():
        arrived(kv_recv.at[0], kv_rs.at[0])

    @pl.when(KV_HEADS + t // 2 != t)
    def _():
        arrived(kv_recv.at[1], kv_rs.at[1])

    queries = q_all[t].astype(F32)
    token_key = kv_recv[0].astype(F32)
    token_value = kv_recv[1].astype(F32)
    token_score = jnp.zeros((REQ, 128), F32)
    for j in range(4):
        product = queries[:, j // 2 * 128 : j // 2 * 128 + 128] * token_key
        product = jnp.where(low_half if j % 2 == 0 else jnp.logical_not(low_half), product, 0.0)
        token_score = jnp.where(lane16 == 6 * j, jnp.sum(product, axis=-1, keepdims=True), token_score)

    part_recv[t] = part_send[t]
    arrived(part_recv.at[pl.ds(0, 7)], z_recv.at[1])

    maxima, totals = [], []
    for s in range(8):
        stat = part_recv[s, :, 256:384].astype(F32)
        stat = stat + pltpu.roll(stat, 127, 1) + pltpu.roll(stat, 126, 1)
        maxima.append(stat)
        totals.append(pltpu.roll(stat, 125, 1))
    upper = token_score
    for entry in maxima:
        upper = jnp.maximum(upper, entry)
    fresh = jnp.exp(token_score - upper)
    total = fresh
    factors = []
    for entry, share in zip(maxima, totals):
        factors.append(jnp.exp(entry - upper))
        total = total + share * factors[-1]

    def widen(value, b):
        return jnp.where(low_half, value[:, 12 * b : 12 * b + 1], value[:, 12 * b + 6 : 12 * b + 7])

    halves = []
    for b in range(2):
        summed = widen(fresh.astype(BF16).astype(F32), b) * token_value
        for s in range(8):
            summed = summed + part_recv[s, :, 128 * b : 128 * b + 128].astype(F32) * widen(factors[s], b)
        halves.append((summed / widen(total, b)).astype(BF16))
    attention = jnp.concatenate(halves, axis=1)

    locals_[5].wait()
    for d in (4, 3, 5, 2, 6, 1, 7, 0):
        to = (t + d) % 8
        block = dot(attention, v_wo[:, pl.ds(pl.multiple_of(to * 256, 256), 256)]).astype(BF16)
        if d:
            rs_send[to] = block
            send(rs_send.at[to], rs_recv.at[t], z_send.at[2], z_recv.at[2], z_peer[d])
        else:
            rs_recv[t] = block
    arrived(rs_recv.at[pl.ds(0, 7)], z_recv.at[2])
    result = v_hid[:, pl.ds(pl.multiple_of(t * 256, 256), 256)].astype(F32)
    for s in range(8):
        result = result + rs_recv[s].astype(F32)
    out_h[...] = result.astype(BF16)

    arrived(part_send.at[pl.ds(0, 7)], z_send.at[1])
    arrived(rs_send.at[pl.ds(0, 7)], z_send.at[2])
    for j in range(2):
        target = (t % KV_HEADS) * 2 + j

        @pl.when(target != t)
        def _():
            pltpu.make_async_copy(kv_send, kv_send, kv_ss.at[j]).wait()


def on_device(
    hidden_in, norm_gain, w_query, w_keyval, w_output, prefix_cache, private_cache,
    node_parent, node_length, request_node, private_length,
):
    anywhere = pl.BlockSpec(memory_space=pltpu.HBM)
    vector = pl.BlockSpec(memory_space=pltpu.VMEM)
    dma = pltpu.SemaphoreType.DMA
    return pl.pallas_call(
        kernel,
        out_shape=(
            jax.ShapeDtypeStruct((REQ, 256), BF16),
            jax.ShapeDtypeStruct((REQ, HEAD_DIM), BF16),
        ),
        in_specs=[anywhere] * 11,
        out_specs=(vector, vector),
        scratch_shapes=[
            pltpu.VMEM((REQ, 2048), BF16),
            pltpu.VMEM((2048,), BF16),
            pltpu.VMEM((2048, 256), BF16),
            pltpu.VMEM((64, 2048), BF16),
            pltpu.VMEM((256, 2048), BF16),
            pltpu.VMEM((REQ, SLOTS, 512), BF16),
            pltpu.SMEM((64,), jnp.int32),
            pltpu.SMEM((64,), jnp.int32),
            pltpu.SMEM((512,), jnp.int32),
            pltpu.SMEM((REQ,), jnp.int32),
            pltpu.VMEM((64, SLOTS, 512), BF16),
            pltpu.VMEM((8, REQ, 256), BF16),
            pltpu.VMEM((REQ, 128), BF16),
            pltpu.VMEM((2, REQ, 128), BF16),
            pltpu.VMEM((8, REQ, 384), BF16),
            pltpu.VMEM((8, REQ, 384), BF16),
            pltpu.VMEM((8, REQ, 256), BF16),
            pltpu.VMEM((8, REQ, 256), BF16),
            dma((11,)),
            dma,
            dma((2, 4, 4)),
            dma,
            dma,
            dma((3,)),
            dma((3,)),
            dma((2,)),
            dma((2,)),
        ],
        compiler_params=pltpu.CompilerParams(
            collective_id=0, has_side_effects=True, vmem_limit_bytes=40 * 1024 * 1024
        ),
    )(
        *(
            pltpu.with_memory_space_constraint(array, pltpu.HBM)
            for array in (
                hidden_in, norm_gain, w_query, w_keyval.T, w_output, prefix_cache, private_cache,
                node_parent, node_length, request_node, private_length,
            )
        )
    )


def solution(mesh):
    placed = (
        P("grp", None), P(), P(None, "tp"), P(None, "tp"), P("tp", None), P("grp", "tp", None),
        P("grp", "tp", None), P(), P(), P(), P("grp"),
    )
    return jax.shard_map(
        on_device, mesh=mesh, in_specs=placed, out_specs=(P("grp", "tp"), P("grp", "tp")), check_vma=False
    )
```

```python
import math

import jax
import jax.numpy as jnp
from jax import lax
from jax.experimental import pallas as pl
from jax.experimental.pallas import tpu as pltpu
from jax.sharding import PartitionSpec as P

MESH = pl.DeviceIdType.MESH
F32 = jnp.float32
BF16 = jnp.bfloat16
HEADS = 32
KV_HEADS = 4
HEAD_DIM = 64
REQ = 16
SLOTS = 64
ROWS = HEADS * REQ
KW = KV_HEADS * HEAD_DIM
LOW = -1e30


def dot(a, b):
    return jnp.dot(a, b, preferred_element_type=F32)


def dot_t(a, b):
    return lax.dot_general(a, b, (((1,), (1,)), ((), ())), preferred_element_type=F32)


def three_parts(value):
    first = value.astype(BF16).astype(F32)
    rest = value - first
    second = rest.astype(BF16).astype(F32)
    third = (rest - second).astype(BF16).astype(F32)
    return first, second, third


def rope_tables(position):
    lane = lax.broadcasted_iota(jnp.int32, (REQ, 128), 1)
    index = (lane % (HEAD_DIM // 2)).astype(F32)
    frequency = jnp.exp(index * (-2.0 * math.log(10000.0) / HEAD_DIM))
    angle = position * frequency
    front = lane % HEAD_DIM < HEAD_DIM // 2
    sine = jnp.sin(angle)
    return jnp.cos(angle), jnp.where(front, -sine, sine), front


def rope(block, tables):
    cosine, sine, front = tables
    half = HEAD_DIM // 2
    swapped = jnp.where(front, pltpu.roll(block, 128 - half, 1), pltpu.roll(block, half, 1))
    return block * cosine + swapped * sine


def kernel(
    hid, gain, wq, wkv, wo, prefix, private, parent_in, nlen_in, reqnode_in, plen_in,
    out_h, out_kv,
    v_hid, v_gain, v_wq, v_wkv, v_wo, v_priv, parent, nlen, reqnode, plen, nodes,
    q_all, kv_send, kv_recv, part_send, part_recv, rs_send, rs_recv,
    l_sem, d_send, d_recv, s_send, s_recv, z_send, z_recv, kv_ss, kv_rs,
):
    g = lax.axis_index("grp")
    t = lax.axis_index("tp")
    x, y, c = g // 8, (g // 2) % 4, g % 2

    def group(xx, yy, cc):
        return (xx * 4 + yy) * 2 + cc

    def chunk(xx, yy, cc):
        return nodes.at[pl.ds(group(xx, yy, cc) * 2, 2)]

    x_peer = {d: (group((x + 4 + d * (1 - 2 * c)) % 4, y, c), t) for d in (1, 2, -1)}
    y_peer = {d: (group(x, (y + 4 + d * (1 - 2 * c)) % 4, c), t) for d in (1, 2, -1)}
    sibling = (group(x, y, 1 - c), t)
    z_peer = [(g, (t + d) % 8) for d in range(8)]
    everyone = list(x_peer.values()) + list(y_peer.values()) + [sibling] + z_peer[1:]

    barrier = pltpu.get_barrier_semaphore()
    for peer in everyone:
        pl.semaphore_signal(barrier, inc=1, device_id=peer, device_id_type=MESH)

    locals_ = []
    for k, (src, dst) in enumerate(
        ((hid, v_hid), (gain, v_gain), (wq, v_wq), (wkv, v_wkv), (private, v_priv), (wo, v_wo),
         (prefix, chunk(x, y, c)), (parent_in, parent), (nlen_in, nlen), (reqnode_in, reqnode), (plen_in, plen))
    ):
        copy = pltpu.make_async_copy(src, dst, l_sem.at[k])
        if k not in (4, 5, 6):
            copy.start()
        locals_.append(copy)

    def send(src, dst, ssem, rsem, peer):
        pltpu.make_async_remote_copy(
            src_ref=src, dst_ref=dst, send_sem=ssem, recv_sem=rsem, device_id=peer, device_id_type=MESH
        ).start()

    def arrived(ref, sem):
        pltpu.make_async_copy(ref, ref, sem).wait()

    turn = 1 - 2 * c

    def slab(i, a, b):
        return nodes.at[pl.ds(group((x + 16 - turn * a) % 4, (y + 16 - turn * b) % 4, c) * 2 + i, 1)]

    def hand_on(i, a, b, *ways):
        block = prefix.at[pl.ds(i, 1)] if a + b == 0 else slab(i, a, b)
        for axis, step in ways:
            if axis == "s":
                send(block, slab(i, a, b), s_send, s_recv, sibling)
                continue
            aa, bb = ((a + step) % 4, b) if axis == "x" else (a, (b + step) % 4)
            peer = (x_peer if axis == "x" else y_peer)[step]
            send(block, slab(i, a, b), d_send, d_recv.at[i, aa, bb], peer)

    def relay(i, a, b, *ways):
        if i == 1:
            a, b = b, a
            ways = [({"x": "y", "y": "x"}[axis], step) for axis, step in ways]
        if a + b:
            arrived(slab(i, a, b), d_recv.at[i, a, b])
        hand_on(i, a, b, *ways, ("s", 0))

    pl.semaphore_wait(barrier, len(everyone))
    hand_on(0, 0, 0, ("x", 1), ("x", -1))
    hand_on(1, 0, 0, ("y", 1), ("y", -1))
    hand_on(0, 0, 0, ("x", 2))
    hand_on(1, 0, 0, ("y", 2))
    hand_on(0, 0, 0, ("y", 1), ("y", -1), ("s", 0))
    hand_on(1, 0, 0, ("x", 1), ("x", -1), ("s", 0))
    for k in (4, 5, 6):
        locals_[k].start()

    for k in range(7, 11):
        locals_[k].wait()
    mids = [reqnode[g * REQ + r] for r in range(REQ)]
    root = parent[mids[0]]
    root_length = nlen[root]
    row16 = lax.broadcasted_iota(jnp.int32, (REQ, 128), 0)
    lane16 = lax.broadcasted_iota(jnp.int32, (REQ, 128), 1)
    private_length = jnp.zeros((REQ, 128), jnp.int32)
    mid_length = jnp.zeros((REQ, 128), jnp.int32)
    for r in range(REQ):
        private_length = jnp.where(row16 == r, plen[r], private_length)
        mid_length = jnp.where(row16 == r, nlen[mids[r]], mid_length)
    tables = rope_tables((private_length + mid_length + root_length).astype(F32))

    locals_[0].wait()
    locals_[1].wait()
    floats = v_hid[...].astype(F32)
    spread = jnp.mean(floats * floats, axis=-1, keepdims=True)
    normed = (floats * lax.rsqrt(spread + 1e-05) * v_gain[...].reshape(1, 2048).astype(F32)).astype(BF16)
    locals_[2].wait()
    query = dot(normed, v_wq[...])
    for half in range(2):
        piece = rope(query[:, half * 128 : half * 128 + 128], tables).astype(BF16)
        q_all[t, :, half * 128 : half * 128 + 128] = piece * jnp.asarray(HEAD_DIM**-0.5, BF16)
    locals_[3].wait()
    keyval = dot_t(normed, v_wkv[...])
    doubled = jnp.concatenate([keyval, keyval], axis=1)
    keyval = jnp.where(t < KV_HEADS, rope(doubled, tables), doubled).astype(BF16)
    out_kv[...] = keyval[:, :HEAD_DIM]
    kv_send[...] = keyval
    for d in (4, 3, 5, 2, 6, 1, 7):
        send(q_all.at[t], q_all.at[t], z_send.at[0], z_recv.at[0], z_peer[d])
    kind = t // KV_HEADS
    for j in range(2):
        target = (t % KV_HEADS) * 2 + j

        @pl.when(target != t)
        def _():
            pltpu.make_async_remote_copy(
                src_ref=kv_send, dst_ref=kv_recv.at[kind], send_sem=kv_ss.at[j],
                recv_sem=kv_rs.at[kind], device_id=(g, target), device_id_type=MESH,
            ).start()

        @pl.when(target == t)
        def _():
            kv_recv[kind] = kv_send[...]

    def relay_first():
        for a in (1, 3):
            for i in range(2):
                relay(i, a, 0, ("y", 1), ("y", -1))
        for i in range(2):
            relay(i, 2, 0, ("y", 2), ("y", 1), ("y", -1))

    def relay_second():
        for i in range(2):
            relay(i, 0, 1, ("y", 1))
            relay(i, 0, 3)
        for i in range(2):
            relay(i, 1, 1, ("y", 1))
            relay(i, 3, 3, ("y", -1))

    def relay_last():
        for where in ((1, 3), (3, 1), (2, 1), (2, 3), (0, 2), (2, 2), (1, 2), (3, 2)):
            for i in range(2):
                relay(i, *where)
        arrived(nodes.at[pl.ds(0, 32)], s_recv)

    relay_first()

    arrived(q_all.at[pl.ds(0, 7)], z_recv.at[0])
    lane256 = lax.broadcasted_iota(jnp.int32, (REQ, KW), 1)
    pieces = []
    for h in range(HEADS):
        j, k = h % 4, h // 8
        four = q_all[h // 4].astype(F32)
        shift = ((k - j) * HEAD_DIM) % KW
        if shift:
            four = pltpu.roll(four, shift, 1)
        pieces.append(jnp.where(lane256 // HEAD_DIM == k, four, 0.0).astype(BF16))
    blocked = jnp.concatenate(pieces, axis=0)

    relay_second()
    lane3 = lax.broadcasted_iota(jnp.int32, (1, REQ, 128), 2)
    row3 = lax.broadcasted_iota(jnp.int32, (1, REQ, 128), 1)
    slot3 = lane3 % SLOTS + t * SLOTS
    own_half = lane3 // SLOTS == row3 % 2
    shape3 = (HEADS, REQ, 128)

    def pair_mask(pair, half):
        return (row3 // 2 == pair) & half

    def compact(key_quad, half, so_far):
        for q in range(4):
            wide = dot_t(blocked, key_quad(q))
            for e in range(2):
                block = wide[:, e * 128 : e * 128 + 128].reshape(shape3)
                so_far = jnp.where(pair_mask(q * 2 + e, half), block, so_far)
        return so_far

    def weigh(weights, value_quad, half):
        total = None
        for q in range(4):
            wide = jnp.concatenate(
                [
                    jnp.where(pair_mask(q * 2 + e, half), weights, 0.0).astype(BF16).reshape(ROWS, 128)
                    for e in range(2)
                ],
                axis=1,
            )
            term = dot(wide, value_quad(q))
            total = term if total is None else total + term
        return total

    def softmax_part(scores, valid):
        scores = jnp.where(valid, scores, LOW)
        maxima = jnp.max(scores, axis=-1, keepdims=True)
        weights = jnp.where(valid, jnp.exp(scores - maxima), 0.0)
        return weights, maxima, jnp.sum(weights, axis=-1, keepdims=True)

    locals_[4].wait()

    def own_rows(q, lanes):
        return v_priv[q * 4 : q * 4 + 4, :, lanes].reshape(4 * SLOTS, KW)

    keys, values = pl.ds(0, KW), pl.ds(KW, KW)
    scores = compact(lambda q: own_rows(q, keys), own_half, jnp.zeros(shape3, F32))
    valid = own_half & (slot3 < private_length.reshape(1, REQ, 128))
    weights, own_max, own_total = softmax_part(scores, valid)
    own_sum = weigh(weights, lambda q: own_rows(q, values), own_half)

    relay_last()
    locals_[6].wait()

    def node_rows(q, lanes):
        order = (q * 4 + 1, q * 4, q * 4 + 3, q * 4 + 2)
        return jnp.concatenate([nodes[mids[r], :, lanes] for r in order], axis=0)

    root_keys = nodes[root, :, keys]
    root_values = nodes[root, :, values]
    root_scores = dot_t(blocked, jnp.concatenate([root_keys, root_keys], axis=0)).reshape(shape3)
    node_half = jnp.logical_not(own_half)
    scores = compact(lambda q: node_rows(q, keys), node_half, root_scores)
    limit = jnp.where(node_half, mid_length.reshape(1, REQ, 128), root_length)
    weights, tree_max, tree_total = softmax_part(scores, slot3 < limit)
    tree_sum = weigh(weights, lambda q: node_rows(q, values), node_half)
    tree_sum = tree_sum + dot(
        jnp.where(own_half, weights, 0.0).astype(BF16).reshape(ROWS, 128),
        jnp.concatenate([root_values, root_values], axis=0),
    )

    upper = jnp.maximum(own_max, tree_max)
    own_scale, tree_scale = jnp.exp(own_max - upper), jnp.exp(tree_max - upper)
    total = own_total * own_scale + tree_total * tree_scale
    stats = three_parts(upper) + three_parts(total)
    low_half = lane16 < HEAD_DIM
    for p in range(8):
        for b in range(2):
            pair = []
            for e in range(2):
                h = 4 * p + 2 * b + e
                k = h // 8
                rows, lanes = slice(REQ * h, REQ * h + REQ), slice(128 * (k // 2), 128 * (k // 2) + 128)
                piece = own_sum[rows, lanes] * own_scale[h] + tree_sum[rows, lanes] * tree_scale[h]
                pair.append(piece if k % 2 == e else pltpu.roll(piece, HEAD_DIM, 1))
            part_send[p, :, 128 * b : 128 * b + 128] = jnp.where(low_half, *pair).astype(BF16)
        packed = jnp.zeros((REQ, 128), F32)
        for j in range(4):
            for at, part in enumerate(stats):
                packed = jnp.where(lane16 == 6 * j + at, part[4 * p + j], packed)
        part_send[p, :, 256:384] = packed.astype(BF16)
    for d in (4, 3, 5, 2, 6, 1, 7):
        to = (t + d) % 8
        send(part_send.at[to], part_recv.at[t], z_send.at[1], z_recv.at[1], z_peer[d])

    arrived(nodes.at[pl.ds(0, 30)], d_send)
    arrived(nodes.at[pl.ds(0, 32)], s_send)
    arrived(q_all.at[pl.ds(0, 7)], z_send.at[0])
    @pl.when(t // 2 != t)
    def _():
        arrived(kv_recv.at[0], kv_rs.at[0])

    @pl.when(KV_HEADS + t // 2 != t)
    def _():
        arrived(kv_recv.at[1], kv_rs.at[1])

    queries = q_all[t].astype(F32)
    token_key = kv_recv[0].astype(F32)
    token_value = kv_recv[1].astype(F32)
    token_score = jnp.zeros((REQ, 128), F32)
    for j in range(4):
        product = queries[:, j // 2 * 128 : j // 2 * 128 + 128] * token_key
        product = jnp.where(low_half if j % 2 == 0 else jnp.logical_not(low_half), product, 0.0)
        token_score = jnp.where(lane16 == 6 * j, jnp.sum(product, axis=-1, keepdims=True), token_score)

    part_recv[t] = part_send[t]
    arrived(part_recv.at[pl.ds(0, 7)], z_recv.at[1])

    maxima, totals = [], []
    for s in range(8):
        stat = part_recv[s, :, 256:384].astype(F32)
        stat = stat + pltpu.roll(stat, 127, 1) + pltpu.roll(stat, 126, 1)
        maxima.append(stat)
        totals.append(pltpu.roll(stat, 125, 1))
    upper = token_score
    for entry in maxima:
        upper = jnp.maximum(upper, entry)
    fresh = jnp.exp(token_score - upper)
    total = fresh
    factors = []
    for entry, share in zip(maxima, totals):
        factors.append(jnp.exp(entry - upper))
        total = total + share * factors[-1]

    def widen(value, b):
        return jnp.where(low_half, value[:, 12 * b : 12 * b + 1], value[:, 12 * b + 6 : 12 * b + 7])

    halves = []
    for b in range(2):
        summed = widen(fresh.astype(BF16).astype(F32), b) * token_value
        for s in range(8):
            summed = summed + part_recv[s, :, 128 * b : 128 * b + 128].astype(F32) * widen(factors[s], b)
        halves.append((summed / widen(total, b)).astype(BF16))
    attention = jnp.concatenate(halves, axis=1)

    locals_[5].wait()
    for d in (4, 3, 5, 2, 6, 1, 7, 0):
        to = (t + d) % 8
        block = dot(attention, v_wo[:, pl.ds(pl.multiple_of(to * 256, 256), 256)]).astype(BF16)
        if d:
            rs_send[to] = block
            send(rs_send.at[to], rs_recv.at[t], z_send.at[2], z_recv.at[2], z_peer[d])
        else:
            rs_recv[t] = block
    arrived(part_send.at[pl.ds(0, 7)], z_send.at[1])
    arrived(rs_send.at[pl.ds(0, 7)], z_send.at[2])
    arrived(rs_recv.at[pl.ds(0, 7)], z_recv.at[2])
    result = v_hid[:, pl.ds(pl.multiple_of(t * 256, 256), 256)].astype(F32)
    for s in range(8):
        result = result + rs_recv[s].astype(F32)
    out_h[...] = result.astype(BF16)

    for j in range(2):
        target = (t % KV_HEADS) * 2 + j

        @pl.when(target != t)
        def _():
            pltpu.make_async_copy(kv_send, kv_send, kv_ss.at[j]).wait()


def on_device(
    hidden_in, norm_gain, w_query, w_keyval, w_output, prefix_cache, private_cache,
    node_parent, node_length, request_node, private_length,
):
    anywhere = pl.BlockSpec(memory_space=pltpu.HBM)
    vector = pl.BlockSpec(memory_space=pltpu.VMEM)
    dma = pltpu.SemaphoreType.DMA
    return pl.pallas_call(
        kernel,
        out_shape=(
            jax.ShapeDtypeStruct((REQ, 256), BF16),
            jax.ShapeDtypeStruct((REQ, HEAD_DIM), BF16),
        ),
        in_specs=[anywhere] * 11,
        out_specs=(vector, vector),
        scratch_shapes=[
            pltpu.VMEM((REQ, 2048), BF16),
            pltpu.VMEM((2048,), BF16),
            pltpu.VMEM((2048, 256), BF16),
            pltpu.VMEM((64, 2048), BF16),
            pltpu.VMEM((256, 2048), BF16),
            pltpu.VMEM((REQ, SLOTS, 512), BF16),
            pltpu.SMEM((64,), jnp.int32),
            pltpu.SMEM((64,), jnp.int32),
            pltpu.SMEM((512,), jnp.int32),
            pltpu.SMEM((REQ,), jnp.int32),
            pltpu.VMEM((64, SLOTS, 512), BF16),
            pltpu.VMEM((8, REQ, 256), BF16),
            pltpu.VMEM((REQ, 128), BF16),
            pltpu.VMEM((2, REQ, 128), BF16),
            pltpu.VMEM((8, REQ, 384), BF16),
            pltpu.VMEM((8, REQ, 384), BF16),
            pltpu.VMEM((8, REQ, 256), BF16),
            pltpu.VMEM((8, REQ, 256), BF16),
            dma((11,)),
            dma,
            dma((2, 4, 4)),
            dma,
            dma,
            dma((3,)),
            dma((3,)),
            dma((2,)),
            dma((2,)),
        ],
        compiler_params=pltpu.CompilerParams(
            collective_id=0, has_side_effects=True, vmem_limit_bytes=40 * 1024 * 1024
        ),
    )(
        *(
            pltpu.with_memory_space_constraint(array, pltpu.HBM)
            for array in (
                hidden_in, norm_gain, w_query, w_keyval.T, w_output, prefix_cache, private_cache,
                node_parent, node_length, request_node, private_length,
            )
        )
    )


def solution(mesh):
    placed = (
        P("grp", None), P(), P(None, "tp"), P(None, "tp"), P("tp", None), P("grp", "tp", None),
        P("grp", "tp", None), P(), P(), P(), P("grp"),
    )
    return jax.shard_map(
        on_device, mesh=mesh, in_specs=placed, out_specs=(P("grp", "tp"), P("grp", "tp")), check_vma=False
    )
```
